32 devices in a mesh: grp: 4 (over x, core), wide: 8 (over z, y).
Axes of the slice: x: 2, y: 2, z: 4, core: 2. Of those that a mesh axis runs over, the one named last changes fastest.
Arguments:
- tokens: bfloat16 [4096, 768], P(('grp', 'wide')), may hold values from -6 to 6
- frames: bfloat16 [2048, 768], P(('grp', 'wide')), may hold values from -6 to 6
- cotangent: bfloat16 [4096, 768], P(('grp', 'wide')), may hold values from -6 to 6
- item_lengths: int32 [4, 4], P('grp'), may hold values from 1 to 512, 1024 in all within a row
- frame_lengths: int32 [4, 4], P('grp'), may hold values from 1 to 256, 512 in all within a row
- attn_inputs: bfloat16 [768, 2304], P('wide'), may hold values from -0.21875 to 0.21875
- attn_output: bfloat16 [768, 768], P('wide'), may hold values from -1.75 to 1.75
- cross_queries: bfloat16 [768, 768], P('wide'), may hold values from -0.21875 to 0.21875
- cross_memory: bfloat16 [768, 1536], P('wide'), may hold values from -0.21875 to 0.21875
- cross_output: bfloat16 [768, 768], P('wide'), may hold values from -1.75 to 1.75
- mlp_inputs: bfloat16 [768, 3072], P('wide'), may hold values from -0.21875 to 0.21875
- mlp_output: bfloat16 [3072, 768], P('wide'), may hold values from -0.109375 to 0.109375
- norm_gains: bfloat16 [3, 768], P(None, 'wide'), may hold values from 0.5 to 1.5
- bias_rows: bfloat16 [10, 768], P(None, 'wide'), may hold values from -4 to 4
- mlp_bias: bfloat16 [3072], P('wide'), may hold values from -4 to 4
Outputs:
- block_output: bfloat16 [4096, 768], P(('grp', 'wide'))
- grad_tokens: float32 [4096, 768], P(('grp', 'wide'))
- grad_frames: float32 [2048, 768], P(('grp', 'wide'))
- grad_attn_inputs: float32 [768, 2304], P('wide')
- grad_attn_output: float32 [768, 768], P('wide')
- grad_cross_queries: float32 [768, 768], P('wide')
- grad_cross_memory: float32 [768, 1536], P('wide')
- grad_cross_output: float32 [768, 768], P('wide')
- grad_mlp_inputs: float32 [768, 3072], P('wide')
- grad_mlp_output: float32 [3072, 768], P('wide')
- grad_norm_gains: float32 [3, 768], P(None, 'wide')
- grad_bias_rows: float32 [10, 768], P(None, 'wide')
- grad_mlp_bias: float32 [3072], P('wide')
The draws below stay inside these ranges and needn't reach their ends.
Inputs may be any that keep to these rules, and one draw needn't show every extreme that they name: `item_lengths`: row g gives the lengths of the 4 items packed in order into group g's 1024 token slots; they sum to 1024 and the longest is exactly 512. `frame_lengths`: row g gives the frame counts of the 4 items, laid in the same order over group g's 512 frames; they sum to 512 and the largest is exactly 256.
All inputs are finite; a program needn't handle non-finite values.
Results may differ from the reference program's by a relative error of at most 0.03.
Values may be sent and summed in bfloat16 or wider, within the bound.
No kernel may reach another device: no remote copies, remote signals or barrier semaphores. Data moves between devices by JAX's collectives and lax.ppermute only.
A program may use at most 256 MiB of HBM per device.

```python
import math
import jax
import jax.numpy as jnp
import numpy as np
from jax import lax

D = 768
HEADS = 12
FF = 3072
HEAD_DIM = 64
ITEMS = 4
LMAX = 512
FMAX = 256
GROUP_TOKENS = 1024
GROUP_FRAMES = 512
TOKENS = 4096
FRAMES = 2048
N_GRP = 4


def shard_levels(key, extent, split, low, high):
    def one(dim, parts):
        draws = jax.random.uniform(jax.random.fold_in(jax.random.fold_in(key, 6), dim), (parts,), jnp.float32, low / len(split), high / len(split))
        return jnp.repeat(jnp.exp(draws), extent[dim] // parts).reshape((-1,) + (1,) * (len(extent) - dim - 1))

    level = one(*split[0])
    for cut in split[1:]:
        level = level * one(*cut)
    return level


def profile(amount, total, bound, slope):
    portions = [(1 << 20) // math.isqrt(standing ** slope) + 1 for standing in range(2, amount + 1)]
    spare, holding = total - bound - (amount - 1), [1] * (amount - 1)
    while spare > 0:
        movable = [i for i in range(amount - 1) if holding[i] < bound]
        mass, remaining = sum([portions[i] for i in movable]), spare
        for i in movable:
            extra = min(bound - holding[i], max(1, remaining * portions[i] // mass), spare)
            holding[i] = holding[i] + extra
            spare = spare - extra
    return np.array([bound] + holding)


def uneven(stream_key, amount, total, limit, slope):
    if amount == 2:
        one = jax.random.randint(stream_key, (), max(1, total - limit), min(limit, total - 1) + 1)
        return jnp.stack([one, total - one])
    sizes = jnp.asarray(profile(amount, total, limit, slope), jnp.int32)
    couples = (amount - 1) // 2
    giver, receiver = sizes[1:1 + 2 * couples:2], sizes[2:2 + 2 * couples:2]
    slack = jnp.minimum(giver - 1, limit - receiver)
    passed = jax.random.randint(jax.random.fold_in(stream_key, 1), (couples,), 0, 1 << 20) % (slack + 1)
    sizes = sizes.at[1:1 + 2 * couples:2].set(giver - passed).at[2:2 + 2 * couples:2].set(receiver + passed)
    return sizes[jax.random.permutation(jax.random.fold_in(stream_key, 2), amount)]


def noise(own_key, dims, scale, most, pieces=(), kind=jnp.bfloat16):
    values = scale * jax.random.normal(own_key, dims, jnp.float32)
    if pieces:
        values = values * shard_levels(own_key, dims, pieces, -0.22, 0.18)
    return jnp.clip(values, -most, most).astype(kind)


def setup_inputs(seed: int = 0) -> dict:
    arg_keys = jax.random.split(jax.random.key(seed), 16)
    return {
        "tokens": noise(arg_keys[0], (TOKENS, D), 1.0, 6.0, ((0, 32),)),
        "frames": noise(arg_keys[1], (FRAMES, D), 1.0, 6.0, ((0, 32),)),
        "cotangent": noise(arg_keys[2], (TOKENS, D), 1.0, 6.0, ((0, 32),)),
        "item_lengths": jax.vmap(lambda own: uneven(own, ITEMS, GROUP_TOKENS, LMAX, 2))(jax.random.split(arg_keys[3], N_GRP)).reshape((N_GRP, ITEMS)).astype(jnp.int32),
        "frame_lengths": jax.vmap(lambda own: uneven(own, ITEMS, GROUP_FRAMES, FMAX, 2))(jax.random.split(arg_keys[4], N_GRP)).reshape((N_GRP, ITEMS)).astype(jnp.int32),
        "attn_inputs": noise(arg_keys[5], (D, 3 * D), D ** -0.5, 0.21875, ((0, 8),)),
        "attn_output": noise(arg_keys[6], (D, D), (D // 64) ** -0.5, 1.75, ((0, 8),)),
        "cross_queries": noise(arg_keys[7], (D, D), D ** -0.5, 0.21875, ((0, 8),)),
        "cross_memory": noise(arg_keys[8], (D, 2 * D), D ** -0.5, 0.21875, ((0, 8),)),
        "cross_output": noise(arg_keys[9], (D, D), (D // 64) ** -0.5, 1.75, ((0, 8),)),
        "mlp_inputs": noise(arg_keys[10], (D, FF), D ** -0.5, 0.21875, ((0, 8),)),
        "mlp_output": noise(arg_keys[11], (FF, D), FF ** -0.5, 0.109375, ((0, 8),)),
        "norm_gains": jnp.clip(1.0 + 0.1 * jax.random.normal(arg_keys[12], (3, D), jnp.float32), 0.5, 1.5).astype(jnp.bfloat16),
        "bias_rows": noise(arg_keys[13], (10, D), 0.3, 4.0, ((1, 8),)),
        "mlp_bias": noise(arg_keys[14], (FF,), 0.3, 4.0, ((0, 8),)),
    }


EPSILON = 1e-05
MASKED = -1e+30

@jax.custom_vjp
def low(v):
    return lax.optimization_barrier(v.astype(jnp.bfloat16)).astype(jnp.float32)

@jax.custom_vjp
def low_back(v):
    return v

def low_keep(v):
    return (low(v), None)

def low_pass(kept, grad):
    return (grad,)

def back_keep(v):
    return (v, None)

def back_low(kept, grad):
    return (low(grad),)
low.defvjp(low_keep, low_pass)
low_back.defvjp(back_keep, back_low)

def both_ways(values):
    return low(low_back(values))

def norm_apply(values, gain, shift):
    centre = lax.optimization_barrier(jnp.mean(values, axis=-1, keepdims=True))
    centred = values - centre
    spread = lax.optimization_barrier(jnp.mean(centred * centred, axis=-1, keepdims=True))
    return centred * lax.rsqrt(spread + EPSILON) * gain + shift

def multiply(left_side, right_side):
    return jnp.dot(left_side, right_side, precision=lax.Precision.HIGHEST)

def split_heads(values):
    return values.reshape(values.shape[0], HEADS, HEAD_DIM)

def item_bounds(lengths):
    ends = jnp.cumsum(lengths).astype(jnp.int32)
    return (ends - lengths.astype(jnp.int32), ends)

def place_rows(results, lengths, total_rows):
    starts, ends = item_bounds(lengths)
    positions = jnp.arange(total_rows, dtype=jnp.int32)
    owner = lax.optimization_barrier(jnp.sum((positions[:, None] >= ends[None, :]).astype(jnp.int32), axis=1)).astype(jnp.int32)
    within = positions - jnp.take(starts, owner)
    flat_index = (owner * results.shape[1] + within).astype(jnp.int32)
    return jnp.take(results.reshape(-1, results.shape[2]), flat_index, axis=0)

def self_attention(queries, keys, values, lengths):
    starts, ends = item_bounds(lengths)
    model_width = queries.shape[1]
    filler = jnp.zeros((LMAX, model_width), jnp.float32)
    padded = [jnp.concatenate([array, filler], axis=0) for array in (queries, keys, values)]
    row_pos = jnp.arange(LMAX, dtype=jnp.int32)

    def one_item(item_in):
        first, length = item_in
        window = [split_heads(lax.dynamic_slice_in_dim(array, first.astype(jnp.int32), LMAX, 0)) for array in padded]
        scores = low_back(jnp.einsum('ihd,jhd->hij', window[0], window[1], precision=lax.Precision.HIGHEST) * HEAD_DIM ** (-0.5))
        allowed = (row_pos[None, :] <= row_pos[:, None]) & (row_pos[None, :] < length)
        probs = low(jax.nn.softmax(jnp.where(allowed[None], scores, MASKED), axis=-1))
        return jnp.einsum('hij,jhd->ihd', probs, window[2], precision=lax.Precision.HIGHEST).reshape(LMAX, model_width)
    results = lax.map(jax.checkpoint(one_item), (starts, lengths))
    return place_rows(results, lengths, queries.shape[0])

def cross_attention(queries, memory, lengths, frame_counts):
    starts, ends = item_bounds(lengths)
    frame_starts, frame_ends = item_bounds(frame_counts)
    model_width = queries.shape[1]
    padded_queries = jnp.concatenate([queries, jnp.zeros((LMAX, model_width), jnp.float32)], axis=0)
    padded_memory = jnp.concatenate([memory, jnp.zeros((FMAX, 2 * model_width), jnp.float32)], axis=0)
    column_pos = jnp.arange(FMAX, dtype=jnp.int32)

    def one_item(item_in):
        first, frame_first, frame_count = item_in
        window_q = split_heads(lax.dynamic_slice_in_dim(padded_queries, first.astype(jnp.int32), LMAX, 0))
        window_m = lax.dynamic_slice_in_dim(padded_memory, frame_first.astype(jnp.int32), FMAX, 0)
        keys = split_heads(window_m[:, :model_width])
        values = split_heads(window_m[:, model_width:])
        scores = low_back(jnp.einsum('ihd,jhd->hij', window_q, keys, precision=lax.Precision.HIGHEST) * HEAD_DIM ** (-0.5))
        allowed = column_pos < frame_count
        probs = low(jax.nn.softmax(jnp.where(allowed[None, None, :], scores, MASKED), axis=-1))
        return jnp.einsum('hij,jhd->ihd', probs, values, precision=lax.Precision.HIGHEST).reshape(LMAX, model_width)
    results = lax.map(jax.checkpoint(one_item), (starts, frame_starts, frame_counts))
    return place_rows(results, lengths, queries.shape[0])

def group_forward(weights, token_values, frame_values, lengths, frame_counts):
    attn_inputs, attn_output, cross_queries, cross_memory, cross_output, mlp_inputs, mlp_output, gain_rows, bias_rows, mlp_bias = weights
    zero_row = jnp.zeros((D,), jnp.float32)
    normed_one = low(norm_apply(token_values, gain_rows[0], bias_rows[0]))
    projected = both_ways(multiply(normed_one, attn_inputs) + jnp.concatenate([bias_rows[3], zero_row, bias_rows[4]]))
    attended = both_ways(self_attention(projected[:, :D], projected[:, D:2 * D], projected[:, 2 * D:], lengths))
    after_one = token_values + low_back(multiply(attended, attn_output) + bias_rows[5])
    normed_two = low(norm_apply(after_one, gain_rows[1], bias_rows[1]))
    cross_q = both_ways(multiply(normed_two, cross_queries) + bias_rows[6])
    memory = both_ways(multiply(frame_values, cross_memory) + jnp.concatenate([zero_row, bias_rows[7]]))
    cross_attended = both_ways(cross_attention(cross_q, memory, lengths, frame_counts))
    after_two = after_one + low_back(multiply(cross_attended, cross_output) + bias_rows[8])
    normed_three = low(norm_apply(after_two, gain_rows[2], bias_rows[2]))
    pre_act = low_back(multiply(normed_three, mlp_inputs) + mlp_bias)
    hidden = low(jax.nn.gelu(pre_act, approximate=False))
    return after_two + low_back(multiply(hidden, mlp_output) + bias_rows[9])

def reference(tokens, frames, cotangent, item_lengths, frame_lengths, attn_inputs, attn_output, cross_queries, cross_memory, cross_output, mlp_inputs, mlp_output, norm_gains, bias_rows, mlp_bias):
    params = tuple((array.astype(jnp.float32) for array in (attn_inputs, attn_output, cross_queries, cross_memory, cross_output, mlp_inputs, mlp_output, norm_gains, bias_rows, mlp_bias)))

    def forward(token_values, frame_values, weights):

        def per_group(group_in):
            return group_forward(weights, group_in[0], group_in[1], group_in[2], group_in[3])
        grouped = (token_values.reshape(N_GRP, GROUP_TOKENS, D), frame_values.reshape(N_GRP, GROUP_FRAMES, D), item_lengths, frame_lengths)
        return lax.map(per_group, grouped).reshape(TOKENS, D)
    outputs, pull_back = jax.vjp(forward, tokens.astype(jnp.float32), frames.astype(jnp.float32), params)
    grad_tokens, grad_frames, grads = pull_back(cotangent.astype(jnp.float32))
    return (outputs.astype(jnp.bfloat16), grad_tokens, grad_frames, grads[0], grads[1], grads[2], grads[3], grads[4], grads[5], grads[6], grads[7], grads[8], grads[9])
```

```python
import functools

import jax
import jax.numpy as jnp
from jax import lax
from jax.experimental import pallas as pl
from jax.experimental.pallas import tpu as pltpu
from jax.sharding import PartitionSpec as P

HEADS = 12
HEAD_DIM = 64
LONGEST = 512
EPSILON = 1e-05
MASKED = -1e30
SCALE = HEAD_DIM ** (-0.5)
F32 = jnp.float32
BF16 = jnp.bfloat16
BOTH = ("grp", "wide")
NZ, NY = 4, 2


def dot(left, right):
    return jnp.dot(left, right, preferred_element_type=F32)


def dot_tn(left, right):
    return lax.dot_general(left, right, (((0,), (0,)), ((), ())), preferred_element_type=F32)


def dot_nt(left, right):
    return lax.dot_general(left, right, (((1,), (1,)), ((), ())), preferred_element_type=F32)


def norm_parts(values):
    centre = jnp.mean(values, axis=-1, keepdims=True)
    centred = values - centre
    spread = jnp.mean(centred * centred, axis=-1, keepdims=True)
    inverse = lax.rsqrt(spread + EPSILON)
    return centred * inverse, inverse


def norm_apply(values, gain, shift):
    return norm_parts(values)[0] * gain + shift


def norm_back(values, gain, upstream):
    normal, inverse = norm_parts(values)
    scaled = upstream * gain
    mean_one = jnp.mean(scaled, axis=-1, keepdims=True)
    mean_two = jnp.mean(scaled * normal, axis=-1, keepdims=True)
    grad = inverse * (scaled - mean_one - normal * mean_two)
    return grad, jnp.sum(upstream * normal, axis=0), jnp.sum(upstream, axis=0)


def move(value, wide, dx=0, dc=0, dz=0, dy=0):
    pairs = []
    for x in range(2):
        for c in range(2):
            for z in range(NZ):
                for y in range(NY):
                    source = (x * 2 + c) * wide + z * NY + y
                    target = ((x ^ dx) * 2 + (c ^ dc)) * wide + ((z + dz) % NZ) * NY + (y ^ dy)
                    pairs.append((source, target))
    return lax.ppermute(value, BOTH, pairs)


def shifted(value, wide, by):
    pairs = [(i, i + by) for i in range(wide) if 0 <= i + by < wide]
    return lax.ppermute(value, "wide", pairs)


def pick(value, index, axis):
    return lax.dynamic_index_in_dim(value, index, axis, keepdims=False)


def attention_bias(mode, tok_rows, info_ref, lengths_ref, counts_ref, pos_ref):
    items = lengths_ref.shape[1]
    slot = info_ref[0] * tok_rows + lax.broadcasted_iota(jnp.int32, (tok_rows, 1), 0)
    key = pos_ref[...]
    if mode == "self":
        first = jnp.zeros((tok_rows, 1), jnp.int32)
        start = jnp.int32(0)
        for item in range(items):
            first = jnp.where(slot >= start, start, first)
            start = start + lengths_ref[0, item]
        allowed = (key >= first) & (key <= slot)
    else:
        owner = jnp.zeros((tok_rows, 1), jnp.int32)
        frame_owner = jnp.zeros(key.shape, jnp.int32)
        end = jnp.int32(0)
        frame_end = jnp.int32(0)
        for item in range(items):
            end = end + lengths_ref[0, item]
            frame_end = frame_end + counts_ref[0, item]
            owner = owner + (slot >= end).astype(jnp.int32)
            frame_owner = frame_owner + (key >= frame_end).astype(jnp.int32)
        allowed = owner == frame_owner
    return jnp.where(allowed, 0.0, MASKED).astype(F32)


def softmax_rows(query, keys, bias):
    scores = dot_nt(query, keys) * SCALE + bias
    top = jnp.max(scores, axis=-1, keepdims=True)
    raised = jnp.exp(scores - top)
    return raised / jnp.sum(raised, axis=-1, keepdims=True)


def attention_forward_body(mode, info_ref, lengths_ref, counts_ref, pos_ref, q_ref, kv_ref, out_ref):
    rows, width = q_ref.shape
    bias = attention_bias(mode, rows, info_ref, lengths_ref, counts_ref, pos_ref)
    lane = lax.broadcasted_iota(jnp.int32, (1, 128), 1)

    def pair(number, carry):
        at = pl.ds(pl.multiple_of(number * 128, 128), 128)
        value_at = pl.ds(pl.multiple_of(number * 128 + width, 128), 128)
        query, keys, values = q_ref[:, at], kv_ref[:, at], kv_ref[:, value_at]
        results = []
        for half in range(2):
            keep = (lane // HEAD_DIM == half).astype(BF16)
            probs = softmax_rows(query * keep, keys, bias)
            results.append(dot(probs.astype(BF16), values))
        out_ref[:, at] = jnp.where(lane < HEAD_DIM, results[0], results[1]).astype(BF16)
        return carry

    lax.fori_loop(0, width // 128, pair, 0)


def attention_backward_body(
    mode, info_ref, lengths_ref, counts_ref, pos_ref, q_ref, kv_ref, g_ref, dq_ref, dkv_ref
):
    rows, width = q_ref.shape
    bias = attention_bias(mode, rows, info_ref, lengths_ref, counts_ref, pos_ref)
    lane = lax.broadcasted_iota(jnp.int32, (1, 128), 1)

    def pair(number, carry):
        at = pl.ds(pl.multiple_of(number * 128, 128), 128)
        value_at = pl.ds(pl.multiple_of(number * 128 + width, 128), 128)
        query, keys, values, grads = q_ref[:, at], kv_ref[:, at], kv_ref[:, value_at], g_ref[:, at]
        d_query, d_keys, d_values = [], [], []
        for half in range(2):
            keep = (lane // HEAD_DIM == half).astype(BF16)
            probs = softmax_rows(query * keep, keys, bias)
            d_probs = dot_nt(grads * keep, values)
            delta = jnp.sum(probs * d_probs, axis=-1, keepdims=True)
            d_scores = (probs * (d_probs - delta)).astype(BF16)
            d_query.append(dot(d_scores, keys) * SCALE)
            d_keys.append(dot_tn(d_scores, query) * SCALE)
            d_values.append(dot_tn(probs.astype(BF16), grads))
        first = lane < HEAD_DIM
        dq_ref[:, at] = jnp.where(first, d_query[0], d_query[1]).astype(BF16)
        dkv_ref[:, at] = jnp.where(first, d_keys[0], d_keys[1]).astype(BF16)
        dkv_ref[:, value_at] = jnp.where(first, d_values[0], d_values[1]).astype(BF16)
        return carry

    lax.fori_loop(0, width // 128, pair, 0)


def smem():
    return pl.BlockSpec(memory_space=pltpu.SMEM)


def vmem():
    return pl.BlockSpec(memory_space=pltpu.VMEM)


def attention_forward(mode, info, lengths, counts, positions, query, kv):
    rows, width = query.shape
    count = kv.shape[0]
    return pl.pallas_call(
        functools.partial(attention_forward_body, mode),
        out_shape=jax.ShapeDtypeStruct((rows, width), BF16),
        in_specs=[smem(), smem(), smem(), vmem(), vmem(), vmem()],
        out_specs=vmem(),
        name=mode + "_forward",
        cost_estimate=pl.CostEstimate(
            flops=8 * rows * count * width, bytes_accessed=8 * count * width, transcendentals=rows * count * HEADS
        ),
    )(info, lengths, counts, positions, query, kv)


def attention_backward(mode, info, lengths, counts, positions, query, kv, grads):
    rows, width = query.shape
    count = kv.shape[0]
    return pl.pallas_call(
        functools.partial(attention_backward_body, mode),
        out_shape=(jax.ShapeDtypeStruct((rows, width), BF16), jax.ShapeDtypeStruct(kv.shape, BF16)),
        in_specs=[smem(), smem(), smem(), vmem(), vmem(), vmem(), vmem()],
        out_specs=(vmem(), vmem()),
        name=mode + "_backward",
        cost_estimate=pl.CostEstimate(
            flops=20 * rows * count * width, bytes_accessed=16 * count * width, transcendentals=rows * count * HEADS
        ),
    )(info, lengths, counts, positions, query, kv, grads)


def half_columns(shard, core):
    half = shard.shape[1] // 2
    part = lax.dynamic_slice_in_dim(shard, core * half, half, 1)
    blocks = part.reshape(-1, 96, half)
    return [blocks[i] for i in range(blocks.shape[0])]


def assemble_body(rows, plan, coords_ref, *refs):
    count = len(refs) - len(plan)
    arrays, outs = refs[:count], refs[count:]
    x, c, z, y = coords_ref[0], coords_ref[1], coords_ref[2], coords_ref[3]
    per_core = count // 2
    for number, array in enumerate(arrays):
        core = c ^ (number // per_core)
        local = number % per_core
        row_y = y ^ (local % 2)
        row_x = x ^ (local // 2)

        def step(dz, carry, array=array, core=core, row_y=row_y, row_x=row_x):
            wide = ((z + dz) & (NZ - 1)) * NY + row_y
            cursor = 0
            for out, (blocks, width) in zip(outs, plan):
                half = width // 2
                for block in range(blocks):
                    row = wide * (96 * blocks) + block * 96
                    if rows < 96:
                        row = row + row_x * rows
                    row = pl.multiple_of(row, 16)
                    column = pl.multiple_of(core * half, 128)
                    out[pl.ds(row, rows), pl.ds(column, half)] = array[dz, :, cursor : cursor + half]
                    cursor += half
            return carry

        lax.fori_loop(0, NZ, step, 0)


def gather_weights(shards, coords, wide, use_x):
    x, c, z, y = coords
    own = jnp.concatenate([b for s in shards for b in half_columns(s, c)], axis=1)
    rows = 96
    if use_x:
        rows = 48
        own = lax.dynamic_slice_in_dim(own, x * rows, rows, 0)
    column = jnp.stack([own] + [move(own, wide, dz=-d) for d in range(1, NZ)])
    plane = [column, move(column, wide, dy=1)]
    if use_x:
        plane = plane + [move(v, wide, dx=1) for v in plane]
    arrays = plane + [move(v, wide, dc=1) for v in plane]
    plan = [(s.shape[0] // 96, s.shape[1]) for s in shards]
    return pl.pallas_call(
        functools.partial(assemble_body, rows, plan),
        out_shape=tuple(jax.ShapeDtypeStruct((s.shape[0] * wide, s.shape[1]), BF16) for s in shards),
        in_specs=[smem()] + [vmem()] * len(arrays),
        out_specs=tuple(vmem() for s in shards),
        name="assemble",
        cost_estimate=pl.CostEstimate(
            flops=0, bytes_accessed=sum(4 * s.size * wide for s in shards), transcendentals=0
        ),
    )(jnp.stack(coords).astype(jnp.int32), *arrays)


def scatter_grads(pieces, coords, wide, use_x):
    x, c, z, y = coords

    def joined(parts):
        return parts[0] if len(parts) == 1 else jnp.concatenate(parts, axis=-1)

    if use_x:
        views = [p.reshape(NZ, NY, 2, 48, p.shape[-1]) for p in pieces]
        arrived = move(joined([pick(v, 1 - x, 2) for v in views]), wide, dx=1)
        kept = joined([pick(v, x, 2) for v in views])
        block = (kept.astype(F32) + arrived.astype(F32)).astype(BF16)
        arrived = move(pick(block, 1 - y, 1), wide, dy=1)
        kept = pick(block, y, 1)
    else:
        views = [p.reshape(NZ, NY, 96, p.shape[-1]) for p in pieces]
        arrived = move(joined([pick(v, 1 - y, 1) for v in views]), wide, dy=1)
        kept = joined([pick(v, y, 1) for v in views])
    column = (kept.astype(F32) + arrived.astype(F32)).astype(BF16)
    arrived = [move(pick(column, (z + d) % NZ, 0), wide, dz=d) for d in range(1, NZ)]
    total = pick(column, z, 0).astype(F32)
    for value in arrived:
        total = total + value.astype(F32)
    total = total.astype(BF16)
    other = move(total, wide, dx=1)
    if use_x:
        return jnp.where(x == 0, jnp.concatenate([total, other]), jnp.concatenate([other, total]))
    return (total.astype(F32) + other.astype(F32)).astype(BF16)


def finish_grads(mine, shapes, coords, wide):
    c = coords[1]
    theirs = move(mine, wide, dc=1)
    low = jnp.where(c == 0, mine, theirs)
    high = jnp.where(c == 0, theirs, mine)
    shards, cursor = [], 0
    for rows, width in shapes:
        half = width // 2
        blocks = []
        for block in range(rows // 96):
            at = slice(cursor, cursor + half)
            blocks.append(jnp.concatenate([low[:, at], high[:, at]], axis=1))
            cursor += half
        whole = blocks[0] if len(blocks) == 1 else jnp.concatenate(blocks, axis=0)
        shards.append(whole.astype(F32))
    return shards


def per_device(
    tokens,
    frames,
    cotangent,
    item_lengths,
    frame_lengths,
    attn_inputs,
    attn_output,
    cross_queries,
    cross_memory,
    cross_output,
    mlp_inputs,
    mlp_output,
    norm_gains,
    bias_rows,
    mlp_bias,
):
    width = tokens.shape[1]
    tok_rows = tokens.shape[0]
    frame_rows = frames.shape[0]
    hidden_rows = mlp_output.shape[0]
    wide = lax.axis_size("wide")
    me = lax.axis_index("wide").astype(jnp.int32)
    group = lax.axis_index("grp").astype(jnp.int32)
    span = LONGEST // tok_rows
    fast = wide == NZ * NY
    x, c, z, y = group // 2, group % 2, me // NY, me % NY
    coords = (x, c, z, y)
    part = width // wide

    small = jnp.concatenate([norm_gains.reshape(-1), bias_rows.reshape(-1), mlp_bias])
    window = jnp.concatenate([shifted(tokens, wide, o) for o in range(span, 0, -1)] + [tokens])
    if fast:
        small_rows = -(-small.shape[0] // (16 * width)) * 16
        small = jnp.pad(small, (0, small_rows * width - small.shape[0])).reshape(small_rows, width)
        own = jnp.concatenate([frames, small])
        column = jnp.stack([own] + [move(own, wide, dz=-d) for d in range(1, NZ)])
        plane = jnp.stack([column, move(column, wide, dy=1)])
        all_frames = plane[:, :, :frame_rows].reshape(-1, width)
        number = jnp.arange(wide, dtype=jnp.int32)
        owner = ((z + number % NZ) % NZ) * NY + (y ^ (number // NZ))
        params = plane[:, :, frame_rows:].reshape(NY, NZ, small_rows * width)
        params = jnp.where(y == 0, params, params[::-1])
        params = jnp.roll(params, z, axis=1)
        params = params.transpose(1, 0, 2).reshape(wide, -1)
        w_in, w_out, w_cross_q = gather_weights((attn_inputs, attn_output, cross_queries), coords, wide, False)
        w_memory, w_cross_out = gather_weights((cross_memory, cross_output), coords, wide, True)
        w_mlp_in, w_mlp_out = gather_weights((mlp_inputs, mlp_output), coords, wide, True)
    else:
        gather = functools.partial(lax.all_gather, axis_name="wide", axis=0, tiled=True)
        all_frames = gather(frames)
        owner = jnp.arange(wide, dtype=jnp.int32)
        params = gather(small.reshape(1, -1))
        w_in, w_out, w_cross_q = gather(attn_inputs), gather(attn_output), gather(cross_queries)
        w_memory, w_cross_out = gather(cross_memory), gather(cross_output)
        w_mlp_in, w_mlp_out = gather(mlp_inputs), gather(mlp_output)
    gains = params[:, : 3 * part].reshape(wide, 3, part).transpose(1, 0, 2).reshape(3, width).astype(F32)
    biases = params[:, 3 * part : 13 * part].reshape(wide, 10, part).transpose(1, 0, 2)
    biases = biases.reshape(10, width).astype(F32)
    hidden_bias = params[:, 13 * part : 13 * part + hidden_rows].reshape(-1).astype(F32)
    frame_pos = (owner[:, None] * frame_rows + jnp.arange(frame_rows, dtype=jnp.int32)).reshape(1, -1)
    key_pos = ((me - span) * tok_rows + jnp.arange((span + 1) * tok_rows, dtype=jnp.int32)).reshape(1, -1)
    info = me.reshape(1)
    zero_row = jnp.zeros((width,), F32)

    inputs = tokens.astype(F32)
    normed_window = norm_apply(window.astype(F32), gains[0], biases[0]).astype(BF16)
    normed_one = normed_window[span * tok_rows :]
    query = (dot(normed_one, w_in[:, :width]) + biases[3]).astype(BF16)
    self_kv = (dot(normed_window, w_in[:, width:]) + jnp.concatenate([zero_row, biases[4]])).astype(BF16)
    tables = (info, item_lengths, frame_lengths)
    attended = attention_forward("self", *tables, key_pos, query, self_kv)
    after_one = inputs + dot(attended, w_out) + biases[5]
    normed_two = norm_apply(after_one, gains[1], biases[1]).astype(BF16)
    cross_q = (dot(normed_two, w_cross_q) + biases[6]).astype(BF16)
    memory = (dot(all_frames, w_memory) + jnp.concatenate([zero_row, biases[7]])).astype(BF16)
    cross_att = attention_forward("cross", *tables, frame_pos, cross_q, memory)
    after_two = after_one + dot(cross_att, w_cross_out) + biases[8]
    normed_three = norm_apply(after_two, gains[2], biases[2]).astype(BF16)
    pre_act = dot(normed_three, w_mlp_in) + hidden_bias
    exact_gelu = functools.partial(jax.nn.gelu, approximate=False)
    hidden = exact_gelu(pre_act).astype(BF16)
    block_output = (after_two + dot(hidden, w_mlp_out) + biases[9]).astype(BF16)

    grad_out = cotangent.astype(F32)
    grad_hidden = dot_nt(cotangent, w_mlp_out)
    grad_pre = jax.vjp(exact_gelu, pre_act)[1](grad_hidden)[0].astype(BF16)
    grad_three, gain_three, shift_three = norm_back(after_two, gains[2], dot_nt(grad_pre, w_mlp_in))
    grad_after_two = grad_out + grad_three
    grad_cross_branch = grad_after_two.astype(BF16)
    grad_cross_att = dot_nt(grad_cross_branch, w_cross_out).astype(BF16)
    grad_cross_q, grad_memory = attention_backward(
        "cross", *tables, frame_pos, cross_q, memory, grad_cross_att
    )
    grad_two, gain_two, shift_two = norm_back(after_one, gains[1], dot_nt(grad_cross_q, w_cross_q))
    grad_after_one = grad_after_two + grad_two
    grad_self_branch = grad_after_one.astype(BF16)
    grad_attended = dot_nt(grad_self_branch, w_out).astype(BF16)
    grad_query, grad_kv = attention_backward("self", *tables, key_pos, query, self_kv, grad_attended)

    frame_part = dot_nt(grad_memory, w_memory)
    if fast:
        frame_part = frame_part.astype(BF16).reshape(NY, NZ, frame_rows, width)
        arrived = move(frame_part[1], wide, dy=1)
        line = (frame_part[0].astype(F32) + arrived.astype(F32)).astype(BF16)
        grad_frames = line[0].astype(F32)
        for d in range(1, NZ):
            grad_frames = grad_frames + move(line[d], wide, dz=d).astype(F32)
    else:
        grad_frames = lax.psum_scatter(frame_part, "wide", scatter_dimension=0, tiled=True)

    window_part = dot_nt(grad_kv, w_in[:, width:])
    grad_one = window_part[span * tok_rows :] + dot_nt(grad_query, w_in[:, :width])
    for o in range(1, span + 1):
        block = window_part[(span - o) * tok_rows : (span - o + 1) * tok_rows]
        grad_one = grad_one + shifted(block.astype(BF16), wide, -o).astype(F32)
    grad_first, gain_one, shift_one = norm_back(inputs, gains[0], grad_one)
    grad_tokens = grad_after_one + grad_first

    def total(value):
        return jnp.sum(value.astype(F32), axis=0)

    rows = [
        gain_one,
        gain_two,
        gain_three,
        shift_one,
        shift_two,
        shift_three,
        total(grad_query),
        total(grad_kv[:, width:]),
        total(grad_self_branch),
        total(grad_cross_q),
        total(grad_memory[:, width:]),
        total(grad_cross_branch),
        total(grad_out),
    ]
    pre_total = total(grad_pre)

    if fast:

        def both(value):
            return jnp.concatenate([value, move(value, wide, dc=1)])

        def split(value):
            half = value.shape[1] // 2
            mine = lax.dynamic_slice_in_dim(value, c * half, half, 1)
            theirs = lax.dynamic_slice_in_dim(value, (1 - c) * half, half, 1)
            return jnp.concatenate([mine, move(theirs, wide, dc=1)])

        def weight(left, right):
            grad = dot_tn(left, right).astype(BF16)
            return grad.reshape(wide, -1, 96, grad.shape[1])

        def blocks(grad):
            return [grad[:, i] for i in range(grad.shape[1])]

        half_hidden = weight(both(hidden), split(cotangent))
        half_pre = weight(both(normed_three), split(grad_pre))
        reduced = scatter_grads(blocks(half_pre) + blocks(half_hidden), coords, wide, True)
        g_mlp_in, g_mlp_out = finish_grads(reduced, [mlp_inputs.shape, mlp_output.shape], coords, wide)

        g_cross_out = weight(both(cross_att), split(grad_cross_branch))
        frames_two = both(all_frames)
        g_memory_k = weight(frames_two, split(grad_memory[:, :width]))
        g_memory_v = weight(frames_two, split(grad_memory[:, width:]))
        g_cross_q = weight(both(normed_two), split(grad_cross_q))
        pieces = [p for g in (g_memory_k, g_memory_v, g_cross_out, g_cross_q) for p in blocks(g)]
        reduced = scatter_grads(pieces, coords, wide, False)
        square = (part, width)
        g_memory_k, g_memory_v, g_cross_out, g_cross_q = finish_grads(reduced, [square] * 4, coords, wide)
        g_memory = jnp.concatenate([g_memory_k, g_memory_v], axis=1)

        g_out = weight(both(attended), split(grad_self_branch))
        window_two = both(normed_window)
        g_in_q = weight(both(normed_one), split(grad_query))
        g_in_k = weight(window_two, split(grad_kv[:, :width]))
        g_in_v = weight(window_two, split(grad_kv[:, width:]))
        pieces = [p for g in (g_out, g_in_q, g_in_k, g_in_v) for p in blocks(g)]
        reduced = scatter_grads(pieces, coords, wide, True)
        g_out, g_in_q, g_in_k, g_in_v = finish_grads(reduced, [square] * 4, coords, wide)
        g_in = jnp.concatenate([g_in_q, g_in_k, g_in_v], axis=1)

        small = jnp.concatenate([jnp.stack(rows), pre_total.reshape(-1, width)])
        small = small + move(small, wide, dc=1)
        small = small + move(small, wide, dx=1)
        small = small + move(small, wide, dy=1)
        arrived = [move(small, wide, dz=d) for d in range(1, NZ)]
        small = small + arrived[0] + arrived[1] + arrived[2]
        rows_all = lax.dynamic_slice_in_dim(small[:13], me * part, part, 1)
        g_bias = lax.dynamic_slice_in_dim(small[13:].reshape(-1), me * hidden_rows, hidden_rows, 0)
    else:

        def weight(left, right):
            grad = lax.psum_scatter(dot_tn(left, right), "wide", scatter_dimension=0, tiled=True)
            return lax.psum(grad.astype(BF16), "grp").astype(F32)

        g_in = jnp.concatenate([weight(normed_one, grad_query), weight(normed_window, grad_kv)], axis=1)
        g_out = weight(attended, grad_self_branch)
        g_cross_q = weight(normed_two, grad_cross_q)
        g_memory = weight(all_frames, grad_memory)
        g_cross_out = weight(cross_att, grad_cross_branch)
        g_mlp_in = weight(normed_three, grad_pre)
        g_mlp_out = weight(hidden, cotangent)
        small = lax.psum(jnp.stack(rows), BOTH)
        rows_all = lax.dynamic_slice_in_dim(small, me * part, part, 1)
        g_bias = lax.dynamic_slice_in_dim(lax.psum(pre_total, BOTH), me * hidden_rows, hidden_rows, 0)
    return (
        block_output,
        grad_tokens,
        grad_frames,
        g_in,
        g_out,
        g_cross_q,
        g_memory,
        g_cross_out,
        g_mlp_in,
        g_mlp_out,
        rows_all[:3],
        rows_all[3:],
        g_bias,
    )


def solution(mesh):
    rows = P(BOTH, None)
    weight = P("wide", None)
    columns = P(None, "wide")
    return jax.shard_map(
        per_device,
        mesh=mesh,
        in_specs=(rows,) * 3 + (P("grp", None),) * 2 + (weight,) * 7 + (columns, columns, P("wide")),
        out_specs=(rows,) * 3 + (weight,) * 7 + (columns, columns, P("wide")),
        check_vma=False,
    )
```

```python
import functools

import jax
import jax.numpy as jnp
from jax import lax
from jax.experimental import pallas as pl
from jax.experimental.pallas import tpu as pltpu
from jax.sharding import PartitionSpec as P

HEADS = 12
HEAD_DIM = 64
LONGEST = 512
EPSILON = 1e-05
MASKED = -1e30
SCALE = HEAD_DIM ** (-0.5)
F32 = jnp.float32
BF16 = jnp.bfloat16
BOTH = ("grp", "wide")
NZ, NY = 4, 2


def dot(left, right):
    return jnp.dot(left, right, preferred_element_type=F32)


def dot_tn(left, right):
    return lax.dot_general(left, right, (((0,), (0,)), ((), ())), preferred_element_type=F32)


def dot_nt(left, right):
    return lax.dot_general(left, right, (((1,), (1,)), ((), ())), preferred_element_type=F32)


def norm_parts(values):
    centre = jnp.mean(values, axis=-1, keepdims=True)
    centred = values - centre
    spread = jnp.mean(centred * centred, axis=-1, keepdims=True)
    inverse = lax.rsqrt(spread + EPSILON)
    return centred * inverse, inverse


def norm_apply(values, gain, shift):
    return norm_parts(values)[0] * gain + shift


def norm_back(values, gain, upstream):
    normal, inverse = norm_parts(values)
    scaled = upstream * gain
    mean_one = jnp.mean(scaled, axis=-1, keepdims=True)
    mean_two = jnp.mean(scaled * normal, axis=-1, keepdims=True)
    grad = inverse * (scaled - mean_one - normal * mean_two)
    return grad, jnp.sum(upstream * normal, axis=0), jnp.sum(upstream, axis=0)


def move(value, wide, dx=0, dc=0, dz=0, dy=0):
    pairs = []
    for x in range(2):
        for c in range(2):
            for z in range(NZ):
                for y in range(NY):
                    source = (x * 2 + c) * wide + z * NY + y
                    target = ((x ^ dx) * 2 + (c ^ dc)) * wide + ((z + dz) % NZ) * NY + (y ^ dy)
                    pairs.append((source, target))
    return lax.ppermute(value, BOTH, pairs)


def move_mixed(value, wide, turn):
    pairs = []
    for x in range(2):
        for c in range(2):
            dx = int(c == turn)
            for z in range(NZ):
                for y in range(NY):
                    source = (x * 2 + c) * wide + z * NY + y
                    target = ((x ^ dx) * 2 + c) * wide + z * NY + (y ^ 1 ^ dx)
                    pairs.append((source, target))
    return lax.ppermute(value, BOTH, pairs)


def shifted(value, wide, by):
    pairs = [(i, i + by) for i in range(wide) if 0 <= i + by < wide]
    return lax.ppermute(value, "wide", pairs)


def along_z(value, wide, by):
    pairs = []
    for group in range(4):
        for z in range(NZ):
            for y in range(NY):
                if 0 <= z + by < NZ:
                    source = group * wide + z * NY + y
                    pairs.append((source, source + by * NY))
    return lax.ppermute(value, BOTH, pairs)


def pick(value, index, axis):
    return lax.dynamic_index_in_dim(value, index, axis, keepdims=False)


def attention_bias(mode, tok_rows, info_ref, lengths_ref, counts_ref, pos_ref):
    items = lengths_ref.shape[1]
    slot = info_ref[0] * tok_rows + lax.broadcasted_iota(jnp.int32, (tok_rows, 1), 0)
    key = pos_ref[...]
    if mode == "self":
        first = jnp.zeros((tok_rows, 1), jnp.int32)
        start = jnp.int32(0)
        for item in range(items):
            first = jnp.where(slot >= start, start, first)
            start = start + lengths_ref[0, item]
        allowed = (key >= first) & (key <= slot)
    else:
        owner = jnp.zeros((tok_rows, 1), jnp.int32)
        frame_owner = jnp.zeros(key.shape, jnp.int32)
        end = jnp.int32(0)
        frame_end = jnp.int32(0)
        for item in range(items):
            end = end + lengths_ref[0, item]
            frame_end = frame_end + counts_ref[0, item]
            owner = owner + (slot >= end).astype(jnp.int32)
            frame_owner = frame_owner + (key >= frame_end).astype(jnp.int32)
        allowed = owner == frame_owner
    return jnp.where(allowed, 0.0, MASKED).astype(F32)


def softmax_rows(query, keys, bias):
    scores = dot_nt(query, keys) * SCALE + bias
    top = jnp.max(scores, axis=-1, keepdims=True)
    raised = jnp.exp(scores - top)
    return raised / jnp.sum(raised, axis=-1, keepdims=True)


def attention_forward_body(mode, info_ref, lengths_ref, counts_ref, pos_ref, q_ref, kv_ref, out_ref):
    rows, width = q_ref.shape
    bias = attention_bias(mode, rows, info_ref, lengths_ref, counts_ref, pos_ref)
    lane = lax.broadcasted_iota(jnp.int32, (1, 128), 1)

    def pair(number, carry):
        at = pl.ds(pl.multiple_of(number * 128, 128), 128)
        value_at = pl.ds(pl.multiple_of(number * 128 + width, 128), 128)
        query, keys, values = q_ref[:, at], kv_ref[:, at], kv_ref[:, value_at]
        results = []
        for half in range(2):
            keep = (lane // HEAD_DIM == half).astype(BF16)
            probs = softmax_rows(query * keep, keys, bias)
            results.append(dot(probs.astype(BF16), values))
        out_ref[:, at] = jnp.where(lane < HEAD_DIM, results[0], results[1]).astype(BF16)
        return carry

    lax.fori_loop(0, width // 128, pair, 0)


def attention_backward_body(
    mode, info_ref, lengths_ref, counts_ref, pos_ref, q_ref, kv_ref, g_ref, dq_ref, dkv_ref
):
    rows, width = q_ref.shape
    bias = attention_bias(mode, rows, info_ref, lengths_ref, counts_ref, pos_ref)
    lane = lax.broadcasted_iota(jnp.int32, (1, 128), 1)

    def pair(number, carry):
        at = pl.ds(pl.multiple_of(number * 128, 128), 128)
        value_at = pl.ds(pl.multiple_of(number * 128 + width, 128), 128)
        query, keys, values, grads = q_ref[:, at], kv_ref[:, at], kv_ref[:, value_at], g_ref[:, at]
        d_query, d_keys, d_values = [], [], []
        for half in range(2):
            keep = (lane // HEAD_DIM == half).astype(BF16)
            probs = softmax_rows(query * keep, keys, bias)
            d_probs = dot_nt(grads * keep, values)
            delta = jnp.sum(probs * d_probs, axis=-1, keepdims=True)
            d_scores = (probs * (d_probs - delta)).astype(BF16)
            d_query.append(dot(d_scores, keys) * SCALE)
            d_keys.append(dot_tn(d_scores, query) * SCALE)
            d_values.append(dot_tn(probs.astype(BF16), grads))
        first = lane < HEAD_DIM
        dq_ref[:, at] = jnp.where(first, d_query[0], d_query[1]).astype(BF16)
        dkv_ref[:, at] = jnp.where(first, d_keys[0], d_keys[1]).astype(BF16)
        dkv_ref[:, value_at] = jnp.where(first, d_values[0], d_values[1]).astype(BF16)
        return carry

    lax.fori_loop(0, width // 128, pair, 0)


def smem():
    return pl.BlockSpec(memory_space=pltpu.SMEM)


def vmem():
    return pl.BlockSpec(memory_space=pltpu.VMEM)


def attention_forward(mode, info, lengths, counts, positions, query, kv):
    rows, width = query.shape
    count = kv.shape[0]
    return pl.pallas_call(
        functools.partial(attention_forward_body, mode),
        out_shape=jax.ShapeDtypeStruct((rows, width), BF16),
        in_specs=[smem(), smem(), smem(), vmem(), vmem(), vmem()],
        out_specs=vmem(),
        name=mode + "_forward",
        cost_estimate=pl.CostEstimate(flops=0, bytes_accessed=rows * width, transcendentals=0),
    )(info, lengths, counts, positions, query, kv)


def attention_backward(mode, info, lengths, counts, positions, query, kv, grads):
    rows, width = query.shape
    count = kv.shape[0]
    return pl.pallas_call(
        functools.partial(attention_backward_body, mode),
        out_shape=(jax.ShapeDtypeStruct((rows, width), BF16), jax.ShapeDtypeStruct(kv.shape, BF16)),
        in_specs=[smem(), smem(), smem(), vmem(), vmem(), vmem(), vmem()],
        out_specs=(vmem(), vmem()),
        name=mode + "_backward",
        cost_estimate=pl.CostEstimate(flops=0, bytes_accessed=rows * width, transcendentals=0),
    )(info, lengths, counts, positions, query, kv, grads)


def half_columns(shard, core):
    half = shard.shape[1] // 2
    part = lax.dynamic_slice_in_dim(shard, core * half, half, 1)
    blocks = part.reshape(-1, 96, half)
    return [blocks[i] for i in range(blocks.shape[0])]


def assemble_copies(plan, coords_ref, arrays, outs, sems, spot):
    x, c, z, y = coords_ref[0], coords_ref[1], coords_ref[2], coords_ref[3]
    k, dz = spot // NZ, spot % NZ
    copies = []
    per_spot = len(arrays) * sum(blocks for blocks, _ in plan)
    for number, array in enumerate(arrays):
        core = c ^ (number // 2)
        if number % 2 == 0:
            row_x, row_y = x ^ (k & (1 - core)), y ^ (k & core)
        else:
            row_x, row_y = x ^ (k | core), y ^ (k | (1 - core))
        wide = ((z + dz) & (NZ - 1)) * NY + row_y
        cursor = 0
        for out, (blocks, width) in zip(outs, plan):
            half = width // 2
            for block in range(blocks):
                row = pl.multiple_of(wide * (96 * blocks) + block * 96 + row_x * 48, 16)
                column = pl.multiple_of(core * half, 128)
                copies.append(
                    pltpu.make_async_copy(
                        array.at[k, dz, :, pl.ds(cursor, half)],
                        out.at[pl.ds(row, 48), pl.ds(column, half)],
                        sems.at[spot * per_spot + len(copies)],
                    )
                )
                cursor += half
    return copies


def assemble_body(plan, coords_ref, *refs):
    arrays, outs, sems = refs[:4], refs[4:-1], refs[-1]

    def start(spot, carry):
        for copy in assemble_copies(plan, coords_ref, arrays, outs, sems, spot):
            copy.start()
        return carry

    def wait(spot, carry):
        for copy in assemble_copies(plan, coords_ref, arrays, outs, sems, spot):
            copy.wait()
        return carry

    lax.fori_loop(0, 2 * NZ, start, 0)
    lax.fori_loop(0, 2 * NZ, wait, 0)


def gather_weights(shards, coords, wide, after=None):
    x, c, z, y = coords
    own = jnp.concatenate([b for s in shards for b in half_columns(s, c)], axis=1)
    own = lax.dynamic_slice_in_dim(own, x * 48, 48, 0)
    if after is not None:
        own, after = lax.optimization_barrier((own, after))
    column = jnp.stack([own] + [move(own, wide, dz=-d) for d in range(1, NZ)])
    pair = jnp.stack([column, move_mixed(column, wide, 0)])
    far = move_mixed(pair, wide, 1)
    arrays = [pair, far, move(pair, wide, dc=1), move(far, wide, dc=1)]
    plan = [(s.shape[0] // 96, s.shape[1]) for s in shards]
    return pl.pallas_call(
        functools.partial(assemble_body, plan),
        out_shape=tuple(jax.ShapeDtypeStruct((s.shape[0] * wide, s.shape[1]), BF16) for s in shards),
        in_specs=[smem()] + [pl.BlockSpec(memory_space=pl.ANY)] * len(arrays),
        out_specs=tuple(vmem() for s in shards),
        scratch_shapes=[pltpu.SemaphoreType.DMA((2 * NZ * 4 * sum(blocks for blocks, _ in plan),))],
        name="assemble",
        cost_estimate=pl.CostEstimate(flops=0, bytes_accessed=sum(s.size for s in shards), transcendentals=0),
    )(jnp.stack(coords).astype(jnp.int32), *arrays)


def joined(parts):
    return parts[0] if len(parts) == 1 else jnp.concatenate(parts, axis=-1)


def added(kept, arrived):
    return (kept.astype(F32) + arrived.astype(F32)).astype(BF16)


def scatter_steps(pieces, coords, wide):
    x, c, z, y = coords
    views = [p.reshape(NZ, NY, 2, 48, p.shape[-1]) for p in pieces]
    send = joined([jnp.where(c == 0, pick(v, 1 - x, 2), pick(v, 1 - y, 1)) for v in views])
    keep = joined([jnp.where(c == 0, pick(v, x, 2), pick(v, y, 1)) for v in views])
    send, keep = yield send, keep
    block = added(keep, move_mixed(send, wide, 0))
    own = jnp.where(c == 0, y, x)
    send, keep = pick(block, 1 - own, 1), pick(block, own, 1)
    send, keep = yield send, keep
    column = added(keep, move_mixed(send, wide, 1))
    column = yield column
    arrived = [move(pick(column, (z + d) % NZ, 0), wide, dz=d) for d in range(1, NZ)]
    total = pick(column, z, 0).astype(F32)
    for value in arrived:
        total = total + value.astype(F32)
    total = total.astype(BF16)
    total = yield total
    other = move(total, wide, dx=1)
    return jnp.where(x == 0, jnp.concatenate([total, other]), jnp.concatenate([other, total]))


class Chain:
    def __init__(self, steps):
        self.steps = steps
        self.held = next(steps)
        self.result = None

    def go(self, value):
        held, value = lax.optimization_barrier((self.held, value))
        try:
            self.held = self.steps.send(held)
        except StopIteration as stop:
            self.result = stop.value
        return value

    def finish(self):
        while self.result is None:
            try:
                self.held = self.steps.send(self.held)
            except StopIteration as stop:
                self.result = stop.value
        return self.result


def finish_grads(mine, shapes, coords, wide):
    c = coords[1]
    theirs = move(mine, wide, dc=1)
    low = jnp.where(c == 0, mine, theirs)
    high = jnp.where(c == 0, theirs, mine)
    shards, cursor = [], 0
    for rows, width in shapes:
        half = width // 2
        blocks = []
        for block in range(rows // 96):
            at = slice(cursor, cursor + half)
            blocks.append(jnp.concatenate([low[:, at], high[:, at]], axis=1))
            cursor += half
        whole = blocks[0] if len(blocks) == 1 else jnp.concatenate(blocks, axis=0)
        shards.append(whole.astype(F32))
    return shards


def per_device(
    tokens,
    frames,
    cotangent,
    item_lengths,
    frame_lengths,
    attn_inputs,
    attn_output,
    cross_queries,
    cross_memory,
    cross_output,
    mlp_inputs,
    mlp_output,
    norm_gains,
    bias_rows,
    mlp_bias,
):
    width = tokens.shape[1]
    tok_rows = tokens.shape[0]
    frame_rows = frames.shape[0]
    hidden_rows = mlp_output.shape[0]
    wide = lax.axis_size("wide")
    me = lax.axis_index("wide").astype(jnp.int32)
    group = lax.axis_index("grp").astype(jnp.int32)
    span = LONGEST // tok_rows
    fast = wide == NZ * NY
    x, c, z, y = group // 2, group % 2, me // NY, me % NY
    coords = (x, c, z, y)
    part = width // wide

    small = jnp.concatenate([norm_gains.reshape(-1), bias_rows.reshape(-1), mlp_bias])
    if fast:
        small_rows = -(-small.shape[0] // (16 * width)) * 16
        small = jnp.pad(small, (0, small_rows * width - small.shape[0])).reshape(small_rows, width)
        own = jnp.concatenate([frames, small])
        reach = -(-span // NY)
        line = [own] + [move(own, wide, dz=-d) for d in range(1, NZ)]
        earlier = [tokens] + [along_z(tokens, wide, d) for d in range(1, reach + 1)]
        line = jnp.concatenate(line + earlier)
        plane = jnp.stack([line, move(line, wide, dy=1)])
        columns = plane[:, : NZ * (frame_rows + small_rows)].reshape(NY, NZ, -1, width)
        all_frames = columns[:, :, :frame_rows].reshape(-1, width)
        number = jnp.arange(wide, dtype=jnp.int32)
        owner = ((z + number % NZ) % NZ) * NY + (y ^ (number // NZ))
        params = columns[:, :, frame_rows:].reshape(NY, NZ, small_rows * width)
        params = jnp.where(y == 0, jnp.stack([params[0], params[1]], 1), jnp.stack([params[1], params[0]], 1))
        params = jnp.concatenate([params, params])
        params = lax.dynamic_slice_in_dim(params, (NZ - z) % NZ, NZ, 0).reshape(wide, -1)
        window = plane[:, NZ * (frame_rows + small_rows) :].reshape(-1, width)
        blocks_at = jnp.array([NY * d for d in range(reach + 1)], jnp.int32)
        blocks_at = jnp.concatenate([me - blocks_at, (z * NY + (1 - y)) - blocks_at])
        w_in, w_out, w_cross_q, w_memory, w_cross_out = gather_weights(
            (attn_inputs, attn_output, cross_queries, cross_memory, cross_output), coords, wide
        )
        w_mlp_in, w_mlp_out = gather_weights((mlp_inputs, mlp_output), coords, wide)
    else:
        gather = functools.partial(lax.all_gather, axis_name="wide", axis=0, tiled=True)
        window = jnp.concatenate([tokens] + [shifted(tokens, wide, o) for o in range(1, span + 1)])
        blocks_at = me - jnp.arange(span + 1, dtype=jnp.int32)
        all_frames = gather(frames)
        owner = jnp.arange(wide, dtype=jnp.int32)
        params = gather(small.reshape(1, -1))
        w_in, w_out, w_cross_q = gather(attn_inputs), gather(attn_output), gather(cross_queries)
        w_memory, w_cross_out = gather(cross_memory), gather(cross_output)
        w_mlp_in, w_mlp_out = gather(mlp_inputs), gather(mlp_output)
    gains = params[:, : 3 * part].reshape(wide, 3, part).transpose(1, 0, 2).reshape(3, width).astype(F32)
    biases = params[:, 3 * part : 13 * part].reshape(wide, 10, part).transpose(1, 0, 2)
    biases = biases.reshape(10, width).astype(F32)
    hidden_bias = params[:, 13 * part : 13 * part + hidden_rows].reshape(-1).astype(F32)
    frame_pos = (owner[:, None] * frame_rows + jnp.arange(frame_rows, dtype=jnp.int32)).reshape(1, -1)
    key_pos = (blocks_at[:, None] * tok_rows + jnp.arange(tok_rows, dtype=jnp.int32)).reshape(1, -1)
    info = me.reshape(1)
    zero_row = jnp.zeros((width,), F32)

    def swapped(parts):
        theirs = move(jnp.concatenate(parts), wide, dc=1)
        found, cursor = [], 0
        for value in parts:
            found.append(theirs[cursor : cursor + value.shape[0]])
            cursor += value.shape[0]
        return found

    def halves(values):
        half = values[0].shape[1] // 2
        mine = [lax.dynamic_slice_in_dim(v, c * half, half, 1) for v in values]
        theirs = swapped([lax.dynamic_slice_in_dim(v, (1 - c) * half, half, 1) for v in values])
        return [jnp.concatenate(pair) for pair in zip(mine, theirs)]

    def doubled(values):
        return [jnp.concatenate(pair) for pair in zip(values, swapped(values))]

    def weight(left, right):
        grad = dot_tn(left, right).astype(BF16)
        return grad.reshape(wide, -1, 96, grad.shape[1])

    def blocks(*grads):
        return [grad[:, i] for grad in grads for i in range(grad.shape[1])]

    inputs = tokens.astype(F32)
    normal_window = norm_parts(window.astype(F32))[0]
    normed_window = (normal_window * gains[0] + biases[0]).astype(BF16)
    normed_one = normed_window[:tok_rows]
    query = (dot(normed_one, w_in[:, :width]) + biases[3]).astype(BF16)
    self_kv = (dot(normed_window, w_in[:, width:]) + jnp.concatenate([zero_row, biases[4]])).astype(BF16)
    tables = (info, item_lengths, frame_lengths)
    attended = attention_forward("self", *tables, key_pos, query, self_kv)
    after_one = inputs + dot(attended, w_out) + biases[5]
    normed_two = norm_apply(after_one, gains[1], biases[1]).astype(BF16)
    cross_q = (dot(normed_two, w_cross_q) + biases[6]).astype(BF16)
    memory = (dot(all_frames, w_memory) + jnp.concatenate([zero_row, biases[7]])).astype(BF16)
    cross_att = attention_forward("cross", *tables, frame_pos, cross_q, memory)
    after_two = after_one + dot(cross_att, w_cross_out) + biases[8]
    normed_three = norm_apply(after_two, gains[2], biases[2]).astype(BF16)
    pre_act = dot(normed_three, w_mlp_in) + hidden_bias
    exact_gelu = functools.partial(jax.nn.gelu, approximate=False)
    hidden = exact_gelu(pre_act).astype(BF16)
    block_output = (after_two + dot(hidden, w_mlp_out) + biases[9]).astype(BF16)

    grad_out = cotangent.astype(F32)
    grad_hidden = dot_nt(cotangent, w_mlp_out)
    grad_pre = jax.vjp(exact_gelu, pre_act)[1](grad_hidden)[0].astype(BF16)
    if fast:
        window_two, frames_two, one_two, attended_two, two_two, cross_att_two, three_two = doubled(
            [normed_window, all_frames, normed_one, attended, normed_two, cross_att, normed_three]
        )
        (hidden_two,) = doubled([hidden])
        (out_half,) = halves([cotangent])
        chain_out = Chain(scatter_steps(blocks(weight(hidden_two, out_half)), coords, wide))
        grad_pre = chain_out.go(grad_pre)
        (pre_half,) = halves([grad_pre])
        chain_in = Chain(scatter_steps(blocks(weight(three_two, pre_half)), coords, wide))
        grad_pre = chain_in.go(grad_pre)
    grad_three, gain_three, shift_three = norm_back(after_two, gains[2], dot_nt(grad_pre, w_mlp_in))
    grad_after_two = grad_out + grad_three
    grad_cross_branch = grad_after_two.astype(BF16)
    grad_cross_att = dot_nt(grad_cross_branch, w_cross_out).astype(BF16)
    grad_cross_q, grad_memory = attention_backward(
        "cross", *tables, frame_pos, cross_q, memory, grad_cross_att
    )
    if fast:
        grad_cross_q = chain_out.go(chain_in.go(grad_cross_q))
    grad_two, gain_two, shift_two = norm_back(after_one, gains[1], dot_nt(grad_cross_q, w_cross_q))
    grad_after_one = grad_after_two + grad_two
    grad_self_branch = grad_after_one.astype(BF16)
    grad_attended = dot_nt(grad_self_branch, w_out).astype(BF16)

    frame_part = dot_nt(grad_memory, w_memory)
    if fast:
        branch_half, cross_half, keys_half, values_half = halves(
            [grad_cross_branch, grad_cross_q, grad_memory[:, :width], grad_memory[:, width:]]
        )
        pieces = blocks(
            weight(frames_two, keys_half),
            weight(frames_two, values_half),
            weight(cross_att_two, branch_half),
            weight(two_two, cross_half),
        )
        chain_cross = Chain(scatter_steps(pieces, coords, wide))
        grad_attended = chain_cross.go(grad_attended)
        frame_part = frame_part.astype(BF16).reshape(NY, NZ, frame_rows, width)
        arrived = move(frame_part[1], wide, dy=1)
        line = added(frame_part[0], arrived)
        grad_frames = line[0].astype(F32)
        for d in range(1, NZ):
            grad_frames = grad_frames + move(line[d], wide, dz=d).astype(F32)
    else:
        grad_frames = lax.psum_scatter(frame_part, "wide", scatter_dimension=0, tiled=True)
    grad_query, grad_kv = attention_backward("self", *tables, key_pos, query, self_kv, grad_attended)
    if fast:
        grad_query = chain_out.go(chain_in.go(grad_query))
        branch_half, query_half, keys_half, values_half = halves(
            [grad_self_branch, grad_query, grad_kv[:, :width], grad_kv[:, width:]]
        )
        grad_in = [weight(one_two, query_half), weight(window_two, keys_half), weight(window_two, values_half)]
        grad_wo = weight(attended_two, branch_half)
        chain_self = Chain(scatter_steps(blocks(*grad_in) + blocks(grad_wo), coords, wide))
        grad_kv = chain_self.go(grad_kv)

    window_part = dot_nt(grad_kv, w_in[:, width:])
    own_part = window_part[:tok_rows] + dot_nt(grad_query, w_in[:, :width])
    window_part = jnp.concatenate([own_part, window_part[tok_rows:]])
    gain_one = jnp.sum(window_part * normal_window, axis=0)
    shift_one = jnp.sum(window_part, axis=0)
    if fast:
        back = window_part.reshape(NY, reach + 1, tok_rows, width)
        arrived = move(back[1].astype(BF16), wide, dy=1).astype(F32)
        line = back[0] + arrived
        grad_one = line[0]
        for d in range(1, reach + 1):
            grad_one = grad_one + along_z(line[d].astype(BF16), wide, -d).astype(F32)
    else:
        grad_one = own_part
        for o in range(1, span + 1):
            block = window_part[o * tok_rows : (o + 1) * tok_rows]
            grad_one = grad_one + shifted(block.astype(BF16), wide, -o).astype(F32)
    grad_tokens = grad_after_one + norm_back(inputs, gains[0], grad_one)[0]

    def total(value):
        return jnp.sum(value.astype(F32), axis=0)

    rows = [
        gain_one,
        gain_two,
        gain_three,
        shift_one,
        shift_two,
        shift_three,
        total(grad_query),
        total(grad_kv[:, width:]),
        total(grad_self_branch),
        total(grad_cross_q),
        total(grad_memory[:, width:]),
        total(grad_cross_branch),
        total(grad_out),
    ]
    pre_total = total(grad_pre)

    if fast:
        extra = pre_total.reshape(wide, -1, part).transpose(1, 0, 2).reshape(-1, width)
        small = jnp.concatenate([jnp.stack(rows), extra])
        small = small + move(small, wide, dc=1)
        small = small + move(small, wide, dx=1)
        small = small + move(small, wide, dy=1)
        arrived = [move(small, wide, dz=d) for d in range(1, NZ)]
        small = small + arrived[0] + arrived[1] + arrived[2]
        small = lax.dynamic_slice_in_dim(small, me * part, part, 1)
        square = (part, width)
        (g_mlp_in,) = finish_grads(chain_in.finish(), [mlp_inputs.shape], coords, wide)
        (g_mlp_out,) = finish_grads(chain_out.finish(), [mlp_output.shape], coords, wide)
        g_memory_k, g_memory_v, g_cross_out, g_cross_q = finish_grads(
            chain_cross.finish(), [square] * 4, coords, wide
        )
        g_in_q, g_in_k, g_in_v, g_out = finish_grads(chain_self.finish(), [square] * 4, coords, wide)
        g_memory = jnp.concatenate([g_memory_k, g_memory_v], axis=1)
        g_in = jnp.concatenate([g_in_q, g_in_k, g_in_v], axis=1)
        rows_all, g_bias = small[:13], small[13:].reshape(-1)
    else:

        def weight_sum(left, right):
            grad = lax.psum_scatter(dot_tn(left, right), "wide", scatter_dimension=0, tiled=True)
            return lax.psum(grad.astype(BF16), "grp").astype(F32)

        g_in = jnp.concatenate(
            [weight_sum(normed_one, grad_query), weight_sum(normed_window, grad_kv)], axis=1
        )
        g_out = weight_sum(attended, grad_self_branch)
        g_cross_q = weight_sum(normed_two, grad_cross_q)
        g_memory = weight_sum(all_frames, grad_memory)
        g_cross_out = weight_sum(cross_att, grad_cross_branch)
        g_mlp_in = weight_sum(normed_three, grad_pre)
        g_mlp_out = weight_sum(hidden, cotangent)
        small = lax.psum(jnp.stack(rows), BOTH)
        rows_all = lax.dynamic_slice_in_dim(small, me * part, part, 1)
        g_bias = lax.dynamic_slice_in_dim(lax.psum(pre_total, BOTH), me * hidden_rows, hidden_rows, 0)
    return (
        block_output,
        grad_tokens,
        grad_frames,
        g_in,
        g_out,
        g_cross_q,
        g_memory,
        g_cross_out,
        g_mlp_in,
        g_mlp_out,
        rows_all[:3],
        rows_all[3:],
        g_bias,
    )


def solution(mesh):
    rows = P(BOTH, None)
    weight = P("wide", None)
    columns = P(None, "wide")
    return jax.shard_map(
        per_device,
        mesh=mesh,
        in_specs=(rows,) * 3 + (P("grp", None),) * 2 + (weight,) * 7 + (columns, columns, P("wide")),
        out_specs=(rows,) * 3 + (weight,) * 7 + (columns, columns, P("wide")),
        check_vma=False,
    )
```

```python
import functools

import jax
import jax.numpy as jnp
from jax import lax
from jax.experimental import pallas as pl
from jax.experimental.pallas import tpu as pltpu
from jax.sharding import PartitionSpec as P

HEADS = 12
HEAD_DIM = 64
LONGEST = 512
EPSILON = 1e-05
MASKED = -1e30
SCALE = HEAD_DIM ** (-0.5)
F32 = jnp.float32
BF16 = jnp.bfloat16
BOTH = ("grp", "wide")
NZ, NY = 4, 2


def dot(left, right):
    return jnp.dot(left, right, preferred_element_type=F32)


def dot_tn(left, right):
    return lax.dot_general(left, right, (((0,), (0,)), ((), ())), preferred_element_type=F32)


def dot_nt(left, right):
    return lax.dot_general(left, right, (((1,), (1,)), ((), ())), preferred_element_type=F32)


def norm_parts(values):
    centre = jnp.mean(values, axis=-1, keepdims=True)
    centred = values - centre
    spread = jnp.mean(centred * centred, axis=-1, keepdims=True)
    inverse = lax.rsqrt(spread + EPSILON)
    return centred * inverse, inverse


def norm_apply(values, gain, shift):
    return norm_parts(values)[0] * gain + shift


def norm_back(values, gain, upstream):
    normal, inverse = norm_parts(values)
    scaled = upstream * gain
    mean_one = jnp.mean(scaled, axis=-1, keepdims=True)
    mean_two = jnp.mean(scaled * normal, axis=-1, keepdims=True)
    grad = inverse * (scaled - mean_one - normal * mean_two)
    return grad, jnp.sum(upstream * normal, axis=0, keepdims=True), jnp.sum(upstream, axis=0, keepdims=True)


def move(value, wide, dx=0, dc=0, dz=0, dy=0):
    pairs = []
    for x in range(2):
        for c in range(2):
            for z in range(NZ):
                for y in range(NY):
                    source = (x * 2 + c) * wide + z * NY + y
                    target = ((x ^ dx) * 2 + (c ^ dc)) * wide + ((z + dz) % NZ) * NY + (y ^ dy)
                    pairs.append((source, target))
    return lax.ppermute(value, BOTH, pairs)


def move_mixed(value, wide, turn):
    pairs = []
    for x in range(2):
        for c in range(2):
            dx = int(c == turn)
            for z in range(NZ):
                for y in range(NY):
                    source = (x * 2 + c) * wide + z * NY + y
                    target = ((x ^ dx) * 2 + c) * wide + z * NY + (y ^ 1 ^ dx)
                    pairs.append((source, target))
    return lax.ppermute(value, BOTH, pairs)


def shifted(value, wide, by):
    pairs = [(i, i + by) for i in range(wide) if 0 <= i + by < wide]
    return lax.ppermute(value, "wide", pairs)


def along_z(value, wide, by):
    pairs = []
    for group in range(4):
        for z in range(NZ):
            for y in range(NY):
                if 0 <= z + by < NZ:
                    source = group * wide + z * NY + y
                    pairs.append((source, source + by * NY))
    return lax.ppermute(value, BOTH, pairs)


def pick(value, index, axis):
    return lax.dynamic_index_in_dim(value, index, axis, keepdims=False)


def attention_bias(mode, tok_rows, info_ref, lengths_ref, counts_ref, pos_ref):
    items = lengths_ref.shape[1]
    slot = info_ref[0] * tok_rows + lax.broadcasted_iota(jnp.int32, (tok_rows, 1), 0)
    key = pos_ref[...]
    if mode == "self":
        first = jnp.zeros((tok_rows, 1), jnp.int32)
        start = jnp.int32(0)
        for item in range(items):
            first = jnp.where(slot >= start, start, first)
            start = start + lengths_ref[0, item]
        allowed = (key >= first) & (key <= slot)
    else:
        owner = jnp.zeros((tok_rows, 1), jnp.int32)
        frame_owner = jnp.zeros(key.shape, jnp.int32)
        end = jnp.int32(0)
        frame_end = jnp.int32(0)
        for item in range(items):
            end = end + lengths_ref[0, item]
            frame_end = frame_end + counts_ref[0, item]
            owner = owner + (slot >= end).astype(jnp.int32)
            frame_owner = frame_owner + (key >= frame_end).astype(jnp.int32)
        allowed = owner == frame_owner
    return jnp.where(allowed, 0.0, MASKED).astype(F32)


def softmax_rows(query, keys, bias):
    scores = dot_nt(query, keys) * SCALE + bias
    top = jnp.max(scores, axis=-1, keepdims=True)
    raised = jnp.exp(scores - top)
    return raised / jnp.sum(raised, axis=-1, keepdims=True)


def attention_forward_body(mode, info_ref, lengths_ref, counts_ref, pos_ref, q_ref, kv_ref, out_ref):
    rows, width = q_ref.shape
    bias = attention_bias(mode, rows, info_ref, lengths_ref, counts_ref, pos_ref)
    lane = lax.broadcasted_iota(jnp.int32, (1, 128), 1)

    def pair(number, carry):
        at = pl.ds(pl.multiple_of(number * 128, 128), 128)
        value_at = pl.ds(pl.multiple_of(number * 128 + width, 128), 128)
        query, keys, values = q_ref[:, at], kv_ref[:, at], kv_ref[:, value_at]
        results = []
        for half in range(2):
            keep = (lane // HEAD_DIM == half).astype(BF16)
            probs = softmax_rows(query * keep, keys, bias)
            results.append(dot(probs.astype(BF16), values))
        out_ref[:, at] = jnp.where(lane < HEAD_DIM, results[0], results[1]).astype(BF16)
        return carry

    lax.fori_loop(0, width // 128, pair, 0)


def attention_backward_body(
    mode, info_ref, lengths_ref, counts_ref, pos_ref, q_ref, kv_ref, g_ref, dq_ref, dkv_ref
):
    rows, width = q_ref.shape
    bias = attention_bias(mode, rows, info_ref, lengths_ref, counts_ref, pos_ref)
    lane = lax.broadcasted_iota(jnp.int32, (1, 128), 1)

    def pair(number, carry):
        at = pl.ds(pl.multiple_of(number * 128, 128), 128)
        value_at = pl.ds(pl.multiple_of(number * 128 + width, 128), 128)
        query, keys, values, grads = q_ref[:, at], kv_ref[:, at], kv_ref[:, value_at], g_ref[:, at]
        d_query, d_keys, d_values = [], [], []
        for half in range(2):
            keep = (lane // HEAD_DIM == half).astype(BF16)
            probs = softmax_rows(query * keep, keys, bias)
            d_probs = dot_nt(grads * keep, values)
            delta = jnp.sum(probs * d_probs, axis=-1, keepdims=True)
            d_scores = (probs * (d_probs - delta)).astype(BF16)
            d_query.append(dot(d_scores, keys) * SCALE)
            d_keys.append(dot_tn(d_scores, query) * SCALE)
            d_values.append(dot_tn(probs.astype(BF16), grads))
        first = lane < HEAD_DIM
        dq_ref[:, at] = jnp.where(first, d_query[0], d_query[1]).astype(BF16)
        dkv_ref[:, at] = jnp.where(first, d_keys[0], d_keys[1]).astype(BF16)
        dkv_ref[:, value_at] = jnp.where(first, d_values[0], d_values[1]).astype(BF16)
        return carry

    lax.fori_loop(0, width // 128, pair, 0)


def smem():
    return pl.BlockSpec(memory_space=pltpu.SMEM)


def vmem():
    return pl.BlockSpec(memory_space=pltpu.VMEM)


def attention_forward(mode, info, lengths, counts, positions, query, kv):
    rows, width = query.shape
    count = kv.shape[0]
    return pl.pallas_call(
        functools.partial(attention_forward_body, mode),
        out_shape=jax.ShapeDtypeStruct((rows, width), BF16),
        in_specs=[smem(), smem(), smem(), vmem(), vmem(), vmem()],
        out_specs=vmem(),
        name=mode + "_forward",
        cost_estimate=pl.CostEstimate(flops=0, bytes_accessed=rows * width, transcendentals=0),
    )(info, lengths, counts, positions, query, kv)


def attention_backward(mode, info, lengths, counts, positions, query, kv, grads):
    rows, width = query.shape
    count = kv.shape[0]
    return pl.pallas_call(
        functools.partial(attention_backward_body, mode),
        out_shape=(jax.ShapeDtypeStruct((rows, width), BF16), jax.ShapeDtypeStruct(kv.shape, BF16)),
        in_specs=[smem(), smem(), smem(), vmem(), vmem(), vmem(), vmem()],
        out_specs=(vmem(), vmem()),
        name=mode + "_backward",
        cost_estimate=pl.CostEstimate(flops=0, bytes_accessed=rows * width, transcendentals=0),
    )(info, lengths, counts, positions, query, kv, grads)


def weight_plan(shards):
    return [(s.shape[0] // 96, s.shape[1]) for s in shards]


def own_body(plan, coords_ref, *refs):
    shards, out, sems = refs[:-2], refs[-2], refs[-1]
    x, c = coords_ref[0], coords_ref[1]
    copies, cursor = [], 0
    for shard, (blocks, width) in zip(shards, plan):
        half = width // 2
        for block in range(blocks):
            row = pl.multiple_of(block * 96 + x * 48, 16)
            column = pl.multiple_of(c * half, 128)
            copies.append(
                pltpu.make_async_copy(
                    shard.at[pl.ds(row, 48), pl.ds(column, half)],
                    out.at[:, pl.ds(cursor, half)],
                    sems.at[len(copies)],
                )
            )
            cursor += half
    for copy in copies:
        copy.start()
    for copy in copies:
        copy.wait()


def own_piece(shards, places):
    plan = weight_plan(shards)
    count = sum(blocks for blocks, _ in plan)
    columns = sum(blocks * width // 2 for blocks, width in plan)
    return pl.pallas_call(
        functools.partial(own_body, plan),
        out_shape=jax.ShapeDtypeStruct((48, columns), BF16),
        in_specs=[smem()] + [pl.BlockSpec(memory_space=pl.ANY)] * len(shards),
        out_specs=vmem(),
        scratch_shapes=[pltpu.SemaphoreType.DMA((count,))],
        name="own_piece",
        cost_estimate=pl.CostEstimate(flops=0, bytes_accessed=48 * columns, transcendentals=0),
    )(places, *shards)


def assemble_copies(plan, straight, coords_ref, arrays, outs, sems, dz):
    x, c, z, y = coords_ref[0], coords_ref[1], coords_ref[2], coords_ref[3]
    copies = []
    per_spot = len(arrays) * sum(blocks for blocks, _ in plan)
    for number, array in enumerate(arrays):
        core = c ^ (number // 4)
        kind = number % 4
        if kind == 0:
            row_x, row_y = x, y
        elif straight:
            row_x, row_y = x ^ (kind // 2), y ^ (kind % 2)
        elif kind == 1:
            row_x, row_y = x ^ (1 - core), y ^ core
        elif kind == 2:
            row_x, row_y = x ^ core, y ^ (1 - core)
        else:
            row_x, row_y = x ^ 1, y ^ 1
        wide = ((z + dz) & (NZ - 1)) * NY + row_y
        cursor = 0
        for out, (blocks, width) in zip(outs, plan):
            half = width // 2
            for block in range(blocks):
                row = pl.multiple_of(wide * (96 * blocks) + block * 96 + row_x * 48, 16)
                column = pl.multiple_of(core * half, 128)
                copies.append(
                    pltpu.make_async_copy(
                        array.at[dz, :, pl.ds(cursor, half)],
                        out.at[pl.ds(row, 48), pl.ds(column, half)],
                        sems.at[dz * per_spot + len(copies)],
                    )
                )
                cursor += half
    return copies


def assemble_body(plan, straight, count, coords_ref, *refs):
    arrays, outs, sems = refs[:count], refs[count:-1], refs[-1]

    def start(dz, carry):
        for copy in assemble_copies(plan, straight, coords_ref, arrays, outs, sems, dz):
            copy.start()
        return carry

    def wait(dz, carry):
        for copy in assemble_copies(plan, straight, coords_ref, arrays, outs, sems, dz):
            copy.wait()
        return carry

    lax.fori_loop(0, NZ, start, 0)
    lax.fori_loop(0, NZ, wait, 0)


def gather_column(own, wide):
    return jnp.stack([own] + [move(own, wide, dz=-d) for d in range(1, NZ)])


def tied(*values):
    return lax.optimization_barrier(values)


def assemble(shards, arrays, straight, places, wide):
    plan = weight_plan(shards)
    return pl.pallas_call(
        functools.partial(assemble_body, plan, straight, len(arrays)),
        out_shape=tuple(jax.ShapeDtypeStruct((s.shape[0] * wide, s.shape[1]), BF16) for s in shards),
        in_specs=[smem()] + [pl.BlockSpec(memory_space=pl.ANY)] * len(arrays),
        out_specs=tuple(vmem() for s in shards),
        scratch_shapes=[pltpu.SemaphoreType.DMA((NZ * len(arrays) * sum(blocks for blocks, _ in plan),))],
        name="assemble",
        cost_estimate=pl.CostEstimate(flops=0, bytes_accessed=sum(s.size for s in shards), transcendentals=0),
    )(places, *arrays)


SMALL = 32


def spread_body(places_ref, frames_ref, gains_ref, biases_ref, hidden_ref, out_ref, slab_ref):
    me = places_ref[2] * NY + places_ref[3]
    rows, width = frames_ref.shape
    count = width // gains_ref.shape[1]
    lane = lax.broadcasted_iota(jnp.int32, (1, width), 1)
    mine = (lane >= me * (width // count)) & (lane < (me + 1) * (width // count))
    slab_ref[...] = jnp.zeros((SMALL, width), F32)
    gains = jnp.concatenate([gains_ref[...].astype(F32)] * count, axis=1)
    slab_ref[0:3, :] = jnp.where(mine, gains, 0.0)
    biases = jnp.concatenate([biases_ref[...].astype(F32)] * count, axis=1)
    slab_ref[3:13, :] = jnp.where(mine, biases, 0.0)
    half = hidden_ref.shape[1]
    hidden = jnp.concatenate([hidden_ref[...].astype(F32)] * (width // half), axis=1)
    side = me % NY
    mine = (lane >= side * half) & (lane < (side + 1) * half)
    hidden = jnp.where(mine, hidden, 0.0)
    for row in range(NZ):
        slab_ref[13 + row : 14 + row, :] = jnp.where(me // NY == row, hidden, 0.0)
    out_ref[0:rows, :] = frames_ref[...]
    out_ref[rows : rows + SMALL, :] = slab_ref[...].astype(BF16)


def spread(places, frames, gains, biases, hidden_bias):
    rows, width = frames.shape
    return pl.pallas_call(
        spread_body,
        out_shape=jax.ShapeDtypeStruct((rows + SMALL, width), BF16),
        in_specs=[smem()] + [vmem()] * 4,
        out_specs=vmem(),
        scratch_shapes=[pltpu.VMEM((SMALL, width), F32)],
        name="spread",
        cost_estimate=pl.CostEstimate(flops=0, bytes_accessed=rows * width, transcendentals=0),
    )(places, frames, gains, biases, hidden_bias.reshape(1, -1))


def collect_body(places_ref, *refs):
    lines, tokens, out_ref = refs[:NZ], refs[NZ:-1], refs[-1]
    y = places_ref[3]
    cursor = 0
    for line in lines:
        out_ref[cursor : cursor + line.shape[0], :] = line[...]
        cursor += line.shape[0]
    for first, second in zip(tokens[:-1], tokens[1:]):
        out_ref[cursor : cursor + first.shape[0], :] = jnp.where(y == 0, first[...], second[...])
        cursor += first.shape[0]


def collect(places, lines, tokens):
    rows = sum(v.shape[0] for v in lines) + sum(v.shape[0] for v in tokens[1:])
    width = lines[0].shape[1]
    return pl.pallas_call(
        collect_body,
        out_shape=jax.ShapeDtypeStruct((rows, width), BF16),
        in_specs=[smem()] + [vmem()] * (len(lines) + len(tokens)),
        out_specs=vmem(),
        name="collect",
        cost_estimate=pl.CostEstimate(flops=0, bytes_accessed=rows * width, transcendentals=0),
    )(places, *lines, *tokens)


def prepare_body(*refs):
    lines, tokens, got_ref = refs[:NZ], refs[NZ : NZ + 3], refs[NZ + 3]
    frames_out, normal_out, normed_out, params_out, self_out, cross_out, hidden_out = refs[NZ + 4 :]
    rows = lines[0].shape[0] - SMALL
    width = lines[0].shape[1]
    small = jnp.zeros((SMALL, width), F32)
    for number in range(NZ):
        small = small + lines[number][rows:, :].astype(F32)
        frames_out[number * rows : (number + 1) * rows, :] = lines[number][:rows, :]
    for number in range(NZ):
        at = number * (rows + SMALL)
        small = small + got_ref[at + rows : at + rows + SMALL, :].astype(F32)
        frames_out[(NZ + number) * rows : (NZ + number + 1) * rows, :] = got_ref[at : at + rows, :]
    params_out[...] = small
    self_out[:, :width] = jnp.zeros((1, width), F32)
    self_out[:, width:] = small[7:8, :]
    cross_out[:, :width] = jnp.zeros((1, width), F32)
    cross_out[:, width:] = small[10:11, :]
    for row in range(NZ):
        hidden_out[:, row * width : (row + 1) * width] = small[13 + row : 14 + row, :]
    gain, shift = small[0:1, :], small[3:4, :]
    step = tokens[0].shape[0]
    at = NZ * (rows + SMALL)
    for number in range(5):
        if number < 3:
            block = tokens[number][...]
        else:
            block = got_ref[at + (number - 3) * step : at + (number - 2) * step, :]
        normal = norm_parts(block.astype(F32))[0]
        normal_out[number * step : (number + 1) * step, :] = normal
        normed_out[number * step : (number + 1) * step, :] = (normal * gain + shift).astype(BF16)


def prepare(lines, tokens, got):
    rows = lines[0].shape[0] - SMALL
    step, width = tokens[0].shape
    shapes = [
        ((2 * NZ * rows, width), BF16),
        ((5 * step, width), F32),
        ((5 * step, width), BF16),
        ((SMALL, width), F32),
        ((1, 2 * width), F32),
        ((1, 2 * width), F32),
        ((1, NZ * width), F32),
    ]
    return pl.pallas_call(
        prepare_body,
        out_shape=tuple(jax.ShapeDtypeStruct(shape, dtype) for shape, dtype in shapes),
        in_specs=[vmem()] * (NZ + 4),
        out_specs=tuple(vmem() for _ in shapes),
        name="prepare",
        cost_estimate=pl.CostEstimate(flops=0, bytes_accessed=got.size, transcendentals=0),
    )(*lines, *tokens, got)


def joined(parts):
    return parts[0] if len(parts) == 1 else jnp.concatenate(parts, axis=-1)


def added(kept, arrived):
    return (kept.astype(F32) + arrived.astype(F32)).astype(BF16)


def scatter_steps(pieces, coords, wide):
    x, c, z, y = coords
    views = [p.reshape(NZ, NY, 2, 48, p.shape[-1]) for p in pieces]
    send = joined([jnp.where(c == 0, pick(v, 1 - x, 2), pick(v, 1 - y, 1)) for v in views])
    keep = joined([jnp.where(c == 0, pick(v, x, 2), pick(v, y, 1)) for v in views])
    send, keep = yield send, keep
    arrived = move_mixed(send, wide, 0)
    keep, arrived = yield keep, arrived
    block = added(keep, arrived)
    own = jnp.where(c == 0, y, x)
    send, keep = pick(block, 1 - own, 1), pick(block, own, 1)
    arrived = move_mixed(send, wide, 1)
    keep, arrived = yield keep, arrived
    column = added(keep, arrived)
    arrived = [move(pick(column, (z + d) % NZ, 0), wide, dz=d) for d in range(1, NZ)]
    total, arrived = yield pick(column, z, 0), arrived
    total = total.astype(F32)
    for value in arrived:
        total = total + value.astype(F32)
    total = total.astype(BF16)
    other = move(total, wide, dx=1)
    total, other = yield total, other
    mine = jnp.where(x == 0, jnp.concatenate([total, other]), jnp.concatenate([other, total]))
    theirs = move(mine, wide, dc=1)
    return mine, theirs


def totals_body(places, slab_given, *refs):
    out_ref = refs[-1]
    if slab_given:
        out_ref[...] = refs[0][...]
    else:
        out_ref[...] = jnp.zeros(out_ref.shape, F32)
    width = out_ref.shape[1]
    for (row, start), ref in zip(places, refs[int(slab_given) : -1]):
        for number in range((ref.shape[1] - start) // width):
            at = start + number * width
            value = ref[:, at : at + width].astype(F32)
            if ref.shape[0] > 1:
                value = jnp.sum(value, axis=0, keepdims=True)
            out_ref[row + number : row + number + 1, :] = value


def totals(entries, width, slab=None):
    given = [] if slab is None else [slab]
    arrays = given + [array for _, array, _ in entries]
    return pl.pallas_call(
        functools.partial(totals_body, [(row, start) for row, _, start in entries], slab is not None),
        out_shape=jax.ShapeDtypeStruct((24, width), F32),
        in_specs=[vmem()] * len(arrays),
        out_specs=vmem(),
        name="totals",
        cost_estimate=pl.CostEstimate(flops=0, bytes_accessed=24 * width, transcendentals=0),
    )(*arrays)


class Chain:
    def __init__(self, steps):
        self.steps = steps
        self.held = next(steps)
        self.result = None

    def go(self, value):
        held, value = lax.optimization_barrier((self.held, value))
        try:
            self.held = self.steps.send(held)
        except StopIteration as stop:
            self.result = stop.value
        return value

    def finish(self):
        while self.result is None:
            try:
                self.held = self.steps.send(self.held)
            except StopIteration as stop:
                self.result = stop.value
        return self.result


def frame_steps(part, wide):
    arrived = move(part[1], wide, dy=1)
    kept, arrived = yield part[0], arrived
    line = added(kept, arrived)
    arrived = [move(line[d], wide, dz=d) for d in range(1, NZ)]
    total, arrived = yield line[0], arrived
    total = total.astype(F32)
    for value in arrived:
        total = total + value.astype(F32)
    return total


def back_steps(back, y, wide):
    arrived = move(back[3:].astype(BF16), wide, dy=1)
    arrived, back = yield arrived, back
    arrived = arrived.astype(F32)
    line = [
        back[0] + jnp.where(y == 0, arrived[0], 0.0),
        back[1] + jnp.where(y == 0, arrived[1], arrived[0]),
        back[2] + jnp.where(y == 0, 0.0, arrived[1]),
    ]
    arrived = [along_z(line[d].astype(BF16), wide, -d) for d in range(1, 3)]
    own, arrived = yield line[0], arrived
    for value in arrived:
        own = own + value.astype(F32)
    return own


def small_steps(slab, wide):
    moves = (
        lambda v: [move(v, wide, dc=1)],
        lambda v: [move_mixed(v, wide, 0)],
        lambda v: [move_mixed(v, wide, 1)],
        lambda v: [move(v, wide, dz=d) for d in range(1, NZ)],
    )
    for step in moves:
        slab, arrived = yield slab, step(slab)
        for value in arrived:
            slab = slab + value
    return slab


def finish_grads(both, shapes, coords):
    c = coords[1]
    mine, theirs = both
    low = jnp.where(c == 0, mine, theirs)
    high = jnp.where(c == 0, theirs, mine)
    shards, cursor = [], 0
    for rows, width in shapes:
        half = width // 2
        blocks = []
        for block in range(rows // 96):
            at = slice(cursor, cursor + half)
            blocks.append(jnp.concatenate([low[:, at], high[:, at]], axis=1))
            cursor += half
        whole = blocks[0] if len(blocks) == 1 else jnp.concatenate(blocks, axis=0)
        shards.append(whole.astype(F32))
    return shards


def per_device(
    tokens,
    frames,
    cotangent,
    item_lengths,
    frame_lengths,
    attn_inputs,
    attn_output,
    cross_queries,
    cross_memory,
    cross_output,
    mlp_inputs,
    mlp_output,
    norm_gains,
    bias_rows,
    mlp_bias,
):
    width = tokens.shape[1]
    tok_rows = tokens.shape[0]
    frame_rows = frames.shape[0]
    hidden_rows = mlp_output.shape[0]
    wide = lax.axis_size("wide")
    me = lax.axis_index("wide").astype(jnp.int32)
    group = lax.axis_index("grp").astype(jnp.int32)
    span = LONGEST // tok_rows
    fast = wide == NZ * NY and span == 4
    x, c, z, y = group // 2, group % 2, me // NY, me % NY
    coords = (x, c, z, y)
    part = width // wide

    early = (attn_inputs, attn_output, cross_queries, cross_memory, cross_output)
    late = (mlp_inputs, mlp_output)
    if fast:
        places = jnp.stack(coords).astype(jnp.int32)
        own_early = own_piece(early, places)
        column_early = gather_column(own_early, wide)
        line = spread(places, frames, norm_gains, bias_rows, mlp_bias)
        own_late = own_piece(late, places)
        column_early, line, blocks_mine, own_late = tied(column_early, line, tokens, own_late)
        via_y = move(column_early, wide, dy=1)
        via_x = move(column_early, wide, dx=1)
        lines = [line] + [move(line, wide, dz=-d) for d in range(1, NZ)]
        blocks_mine = [blocks_mine, along_z(blocks_mine, wide, 1), along_z(blocks_mine, wide, 2)]
        payload = collect(places, lines, blocks_mine)
        payload, via_y, own_late = tied(payload, via_y, own_late)
        far = move(via_y, wide, dx=1)
        got = move(payload, wide, dy=1)
        all_frames, normal_window, normed_window, params, self_bias, cross_bias, hidden_bias = prepare(
            lines, blocks_mine, got
        )
        column_late = gather_column(own_late, wide)
        arrays_early = [column_early, via_y, via_x]
        arrays_early = [move(v, wide, dc=1) for v in arrays_early]
        far, column_late = tied(far, column_late)
        near, side = move_mixed(column_late, wide, 0), move_mixed(column_late, wide, 1)
        arrays_early = [column_early, via_y, via_x, far] + arrays_early + [move(far, wide, dc=1)]
        w_in, w_out, w_cross_q, w_memory, w_cross_out = assemble(early, arrays_early, True, places, wide)
        gains, biases = params[:3], params[3:13]
        number = jnp.arange(wide, dtype=jnp.int32)
        owner = ((z + number % NZ) % NZ) * NY + (y ^ (number // NZ))
        blocks_at = me - jnp.array([0, 2, 4, 1, 3], jnp.int32)
    else:
        gather = functools.partial(lax.all_gather, axis_name="wide", axis=0, tiled=True)
        window = jnp.concatenate([tokens] + [shifted(tokens, wide, o) for o in range(1, span + 1)])
        blocks_at = me - jnp.arange(span + 1, dtype=jnp.int32)
        all_frames = gather(frames)
        owner = jnp.arange(wide, dtype=jnp.int32)
        small = jnp.concatenate([norm_gains.reshape(-1), bias_rows.reshape(-1), mlp_bias])
        params = gather(small.reshape(1, -1))
        w_in, w_out, w_cross_q, w_memory, w_cross_out = [gather(v) for v in early]
        w_mlp_in, w_mlp_out = [gather(v) for v in late]
        gains = params[:, : 3 * part].reshape(wide, 3, part).transpose(1, 0, 2).reshape(3, width).astype(F32)
        biases = params[:, 3 * part : 13 * part].reshape(wide, 10, part).transpose(1, 0, 2)
        biases = biases.reshape(10, width).astype(F32)
        hidden_bias = params[:, 13 * part : 13 * part + hidden_rows].reshape(1, -1).astype(F32)
        zero_row = jnp.zeros((1, width), F32)
        self_bias = jnp.concatenate([zero_row, biases[4:5]], axis=1)
        cross_bias = jnp.concatenate([zero_row, biases[7:8]], axis=1)
        normal_window = norm_parts(window.astype(F32))[0]
        normed_window = (normal_window * gains[:1] + biases[:1]).astype(BF16)
    frame_pos = (owner[:, None] * frame_rows + jnp.arange(frame_rows, dtype=jnp.int32)).reshape(1, -1)
    key_pos = (blocks_at[:, None] * tok_rows + jnp.arange(tok_rows, dtype=jnp.int32)).reshape(1, -1)

    def gain(row):
        return gains[row : row + 1]

    def bias(row):
        return biases[row : row + 1]

    info = me.reshape(1)

    def swapped(parts):
        theirs = move(jnp.concatenate(parts), wide, dc=1)
        found, cursor = [], 0
        for value in parts:
            found.append(theirs[cursor : cursor + value.shape[0]])
            cursor += value.shape[0]
        return found

    def halves(values):
        half = values[0].shape[1] // 2
        mine = [lax.dynamic_slice_in_dim(v, c * half, half, 1) for v in values]
        theirs = swapped([lax.dynamic_slice_in_dim(v, (1 - c) * half, half, 1) for v in values])
        return [jnp.concatenate(pair) for pair in zip(mine, theirs)]

    def doubled(values):
        return [jnp.concatenate(pair) for pair in zip(values, swapped(values))]

    def weight(left, right):
        grad = dot_tn(left, right).astype(BF16)
        return grad.reshape(wide, -1, 96, grad.shape[1])

    def blocks(*grads):
        return [grad[:, i] for grad in grads for i in range(grad.shape[1])]

    inputs = tokens.astype(F32)
    normed_one = normed_window[:tok_rows]
    query = (dot(normed_one, w_in[:, :width]) + bias(3)).astype(BF16)
    self_kv = (dot(normed_window, w_in[:, width:]) + self_bias).astype(BF16)
    tables = (info, item_lengths, frame_lengths)
    attended = attention_forward("self", *tables, key_pos, query, self_kv)
    if fast:
        near, side, attended = tied(near, side, attended)
        arrays_late = [column_late, near, side, move_mixed(near, wide, 1)]
        their_late = [move(v, wide, dc=1) for v in arrays_late[:3]]
    after_one = inputs + dot(attended, w_out) + bias(5)
    normed_two = norm_apply(after_one, gain(1), bias(1)).astype(BF16)
    cross_q = (dot(normed_two, w_cross_q) + bias(6)).astype(BF16)
    memory = (dot(all_frames, w_memory) + cross_bias).astype(BF16)
    cross_att = attention_forward("cross", *tables, frame_pos, cross_q, memory)
    if fast:
        arrays_late[3], cross_att = tied(arrays_late[3], cross_att)
        their_late.append(move(arrays_late[3], wide, dc=1))
        w_mlp_in, w_mlp_out = assemble(late, arrays_late + their_late, False, places, wide)
    after_two = after_one + dot(cross_att, w_cross_out) + bias(8)
    normed_three = norm_apply(after_two, gain(2), bias(2)).astype(BF16)
    pre_act = dot(normed_three, w_mlp_in) + hidden_bias
    exact_gelu = functools.partial(jax.nn.gelu, approximate=False)
    hidden = exact_gelu(pre_act).astype(BF16)
    block_output = (after_two + dot(hidden, w_mlp_out) + bias(9)).astype(BF16)

    grad_out = cotangent.astype(F32)
    grad_hidden = dot_nt(cotangent, w_mlp_out)
    grad_pre = jax.vjp(exact_gelu, pre_act)[1](grad_hidden)[0].astype(BF16)
    if fast:
        window_two, frames_two, attended_two, two_two, cross_att_two, three_two = doubled(
            [normed_window, all_frames, attended, normed_two, cross_att, normed_three]
        )
        rows_two = normed_window.shape[0]
        one_two = jnp.concatenate([window_two[:tok_rows], window_two[rows_two : rows_two + tok_rows]])
        (hidden_two,) = doubled([hidden])
        (out_half,) = halves([cotangent])
        chain_out = Chain(scatter_steps(blocks(weight(hidden_two, out_half)), coords, wide))
        grad_pre = chain_out.go(grad_pre)
        (pre_half,) = halves([grad_pre])
        chain_in = Chain(scatter_steps(blocks(weight(three_two, pre_half)), coords, wide))
        grad_pre = chain_in.go(grad_pre)
    grad_three, gain_three, shift_three = norm_back(after_two, gain(2), dot_nt(grad_pre, w_mlp_in))
    grad_after_two = grad_out + grad_three
    grad_cross_branch = grad_after_two.astype(BF16)
    grad_cross_att = dot_nt(grad_cross_branch, w_cross_out).astype(BF16)
    grad_cross_q, grad_memory = attention_backward(
        "cross", *tables, frame_pos, cross_q, memory, grad_cross_att
    )
    if fast:
        grad_cross_q = chain_out.go(grad_cross_q)
    grad_two, gain_two, shift_two = norm_back(after_one, gain(1), dot_nt(grad_cross_q, w_cross_q))
    grad_after_one = grad_after_two + grad_two
    grad_self_branch = grad_after_one.astype(BF16)
    grad_attended = dot_nt(grad_self_branch, w_out).astype(BF16)

    frame_part = dot_nt(grad_memory, w_memory)
    if fast:
        branch_half, cross_half, keys_half, values_half = halves(
            [grad_cross_branch, grad_cross_q, grad_memory[:, :width], grad_memory[:, width:]]
        )
        pieces = blocks(
            weight(frames_two, keys_half),
            weight(frames_two, values_half),
            weight(cross_att_two, branch_half),
            weight(two_two, cross_half),
        )
        chain_cross = Chain(scatter_steps(pieces, coords, wide))
        frame_part = frame_part.astype(BF16).reshape(NY, NZ, frame_rows, width)
        chain_frames = Chain(frame_steps(frame_part, wide))
        slab = totals(
            [
                (2, gain_three, 0),
                (5, shift_three, 0),
                (1, gain_two, 0),
                (4, shift_two, 0),
                (8, grad_self_branch, 0),
                (9, grad_cross_q, 0),
                (10, grad_memory, width),
                (11, grad_cross_branch, 0),
                (12, cotangent, 0),
                (13, grad_pre, 0),
            ],
            width,
        )
        grad_attended = chain_frames.go(chain_out.go(chain_cross.go(chain_in.go(grad_attended))))
    else:
        grad_frames = lax.psum_scatter(frame_part, "wide", scatter_dimension=0, tiled=True)
    grad_query, grad_kv = attention_backward("self", *tables, key_pos, query, self_kv, grad_attended)
    if fast:
        branch_half, query_half, keys_half, values_half = halves(
            [grad_self_branch, grad_query, grad_kv[:, :width], grad_kv[:, width:]]
        )
        grad_in = [weight(one_two, query_half), weight(window_two, keys_half), weight(window_two, values_half)]
        grad_wo = weight(attended_two, branch_half)
        chain_self = Chain(scatter_steps(blocks(*grad_in) + blocks(grad_wo), coords, wide))
        grad_kv = chain_self.go(grad_kv)

    window_part = dot_nt(grad_kv, w_in[:, width:])
    own_part = window_part[:tok_rows] + dot_nt(grad_query, w_in[:, :width])
    window_part = jnp.concatenate([own_part, window_part[tok_rows:]])
    gain_one = jnp.sum(window_part * normal_window, axis=0, keepdims=True)
    shift_one = jnp.sum(window_part, axis=0, keepdims=True)
    if fast:
        back = window_part.reshape(5, tok_rows, width)
        chain_back = Chain(back_steps(back, y, wide))
        late_rows = [(0, gain_one, 0), (3, shift_one, 0), (6, grad_query, 0), (7, grad_kv, width)]
        chain_small = Chain(small_steps(totals(late_rows, width, slab), wide))
        order = gain_one
        for chain in (
            chain_in,
            chain_out,
            chain_cross,
            chain_small,
            chain_back,
            chain_self,
            chain_cross,
            chain_in,
            chain_small,
            chain_self,
            chain_back,
            chain_cross,
            chain_small,
        ):
            order = chain.go(order)
        grad_one = chain_back.finish()
        grad_frames = chain_frames.finish()
        small = chain_small.finish()
    else:
        grad_one = own_part
        for o in range(1, span + 1):
            block = window_part[o * tok_rows : (o + 1) * tok_rows]
            grad_one = grad_one + shifted(block.astype(BF16), wide, -o).astype(F32)
    grad_tokens = grad_after_one + norm_back(inputs, gain(0), grad_one)[0]

    if fast:
        small_hidden = pick(small[13:17], me // NY, 0)
        small_hidden = lax.dynamic_slice_in_dim(small_hidden, (me % NY) * hidden_rows, hidden_rows, 0)
        small = lax.dynamic_slice_in_dim(small, me * part, part, 1)
        square = (part, width)
        (g_mlp_in,) = finish_grads(chain_in.finish(), [mlp_inputs.shape], coords)
        (g_mlp_out,) = finish_grads(chain_out.finish(), [mlp_output.shape], coords)
        g_memory_k, g_memory_v, g_cross_out, g_cross_q = finish_grads(
            chain_cross.finish(), [square] * 4, coords
        )
        g_in_q, g_in_k, g_in_v, g_out = finish_grads(chain_self.finish(), [square] * 4, coords)
        g_memory = jnp.concatenate([g_memory_k, g_memory_v], axis=1)
        g_in = jnp.concatenate([g_in_q, g_in_k, g_in_v], axis=1)
        rows_all, g_bias = small[:13], small_hidden
    else:

        def weight_sum(left, right):
            grad = lax.psum_scatter(dot_tn(left, right), "wide", scatter_dimension=0, tiled=True)
            return lax.psum(grad.astype(BF16), "grp").astype(F32)

        def total(value):
            return jnp.sum(value.astype(F32), axis=0, keepdims=True)

        rows = [
            gain_one,
            gain_two,
            gain_three,
            shift_one,
            shift_two,
            shift_three,
            total(grad_query),
            total(grad_kv[:, width:]),
            total(grad_self_branch),
            total(grad_cross_q),
            total(grad_memory[:, width:]),
            total(grad_cross_branch),
            total(grad_out),
        ]
        g_in = jnp.concatenate(
            [weight_sum(normed_one, grad_query), weight_sum(normed_window, grad_kv)], axis=1
        )
        g_out = weight_sum(attended, grad_self_branch)
        g_cross_q = weight_sum(normed_two, grad_cross_q)
        g_memory = weight_sum(all_frames, grad_memory)
        g_cross_out = weight_sum(cross_att, grad_cross_branch)
        g_mlp_in = weight_sum(normed_three, grad_pre)
        g_mlp_out = weight_sum(hidden, cotangent)
        small = lax.psum(jnp.concatenate(rows), BOTH)
        rows_all = lax.dynamic_slice_in_dim(small, me * part, part, 1)
        g_bias = lax.psum(total(grad_pre).reshape(-1), BOTH)
        g_bias = lax.dynamic_slice_in_dim(g_bias, me * hidden_rows, hidden_rows, 0)
    return (
        block_output,
        grad_tokens,
        grad_frames,
        g_in,
        g_out,
        g_cross_q,
        g_memory,
        g_cross_out,
        g_mlp_in,
        g_mlp_out,
        rows_all[:3],
        rows_all[3:],
        g_bias,
    )


def solution(mesh):
    rows = P(BOTH, None)
    weight = P("wide", None)
    columns = P(None, "wide")
    return jax.shard_map(
        per_device,
        mesh=mesh,
        in_specs=(rows,) * 3 + (P("grp", None),) * 2 + (weight,) * 7 + (columns, columns, P("wide")),
        out_specs=(rows,) * 3 + (weight,) * 7 + (columns, columns, P("wide")),
        check_vma=False,
    )
```

```python
import functools

import jax
import jax.numpy as jnp
from jax import lax
from jax.experimental import pallas as pl
from jax.experimental.pallas import tpu as pltpu
from jax.sharding import PartitionSpec as P

HEADS = 12
HEAD_DIM = 64
LONGEST = 512
EPSILON = 1e-05
MASKED = -1e30
SCALE = HEAD_DIM ** (-0.5)
F32 = jnp.float32
BF16 = jnp.bfloat16
BOTH = ("grp", "wide")
NZ, NY = 4, 2


def dot(left, right):
    return jnp.dot(left, right, preferred_element_type=F32)


def dot_tn(left, right):
    return lax.dot_general(left, right, (((0,), (0,)), ((), ())), preferred_element_type=F32)


def dot_nt(left, right):
    return lax.dot_general(left, right, (((1,), (1,)), ((), ())), preferred_element_type=F32)


def norm_parts(values):
    centre = jnp.mean(values, axis=-1, keepdims=True)
    centred = values - centre
    spread = jnp.mean(centred * centred, axis=-1, keepdims=True)
    inverse = lax.rsqrt(spread + EPSILON)
    return centred * inverse, inverse


def norm_apply(values, gain, shift):
    return norm_parts(values)[0] * gain + shift


def norm_back(values, gain, upstream):
    normal, inverse = norm_parts(values)
    scaled = upstream * gain
    mean_one = jnp.mean(scaled, axis=-1, keepdims=True)
    mean_two = jnp.mean(scaled * normal, axis=-1, keepdims=True)
    grad = inverse * (scaled - mean_one - normal * mean_two)
    return grad, jnp.sum(upstream * normal, axis=0, keepdims=True), jnp.sum(upstream, axis=0, keepdims=True)


def move(value, wide, dx=0, dc=0, dz=0, dy=0):
    pairs = []
    for x in range(2):
        for c in range(2):
            for z in range(NZ):
                for y in range(NY):
                    source = (x * 2 + c) * wide + z * NY + y
                    target = ((x ^ dx) * 2 + (c ^ dc)) * wide + ((z + dz) % NZ) * NY + (y ^ dy)
                    pairs.append((source, target))
    return lax.ppermute(value, BOTH, pairs)


def move_mixed(value, wide, turn):
    pairs = []
    for x in range(2):
        for c in range(2):
            dx = int(c == turn)
            for z in range(NZ):
                for y in range(NY):
                    source = (x * 2 + c) * wide + z * NY + y
                    target = ((x ^ dx) * 2 + c) * wide + z * NY + (y ^ 1 ^ dx)
                    pairs.append((source, target))
    return lax.ppermute(value, BOTH, pairs)


def shifted(value, wide, by):
    pairs = [(i, i + by) for i in range(wide) if 0 <= i + by < wide]
    return lax.ppermute(value, "wide", pairs)


def along_z(value, wide, by):
    pairs = []
    for group in range(4):
        for z in range(NZ):
            for y in range(NY):
                if 0 <= z + by < NZ:
                    source = group * wide + z * NY + y
                    pairs.append((source, source + by * NY))
    return lax.ppermute(value, BOTH, pairs)


def flip_z(value, wide, bit):
    pairs = []
    for group in range(4):
        for z in range(NZ):
            for y in range(NY):
                pairs.append((group * wide + z * NY + y, group * wide + (z ^ bit) * NY + y))
    return lax.ppermute(value, BOTH, pairs)


def pick(value, index, axis):
    return lax.dynamic_index_in_dim(value, index, axis, keepdims=False)


def attention_bias(mode, tok_rows, info_ref, lengths_ref, counts_ref, pos_ref):
    items = lengths_ref.shape[1]
    slot = info_ref[0] * tok_rows + lax.broadcasted_iota(jnp.int32, (tok_rows, 1), 0)
    key = pos_ref[...]
    if mode == "self":
        first = jnp.zeros((tok_rows, 1), jnp.int32)
        start = jnp.int32(0)
        for item in range(items):
            first = jnp.where(slot >= start, start, first)
            start = start + lengths_ref[0, item]
        allowed = (key >= first) & (key <= slot)
    else:
        owner = jnp.zeros((tok_rows, 1), jnp.int32)
        frame_owner = jnp.zeros(key.shape, jnp.int32)
        end = jnp.int32(0)
        frame_end = jnp.int32(0)
        for item in range(items):
            end = end + lengths_ref[0, item]
            frame_end = frame_end + counts_ref[0, item]
            owner = owner + (slot >= end).astype(jnp.int32)
            frame_owner = frame_owner + (key >= frame_end).astype(jnp.int32)
        allowed = owner == frame_owner
    return jnp.where(allowed, 0.0, MASKED).astype(F32)


def softmax_rows(query, keys, bias):
    scores = dot_nt(query, keys) * SCALE + bias
    top = jnp.max(scores, axis=-1, keepdims=True)
    raised = jnp.exp(scores - top)
    return raised / jnp.sum(raised, axis=-1, keepdims=True)


def attention_forward_body(mode, info_ref, lengths_ref, counts_ref, pos_ref, q_ref, kv_ref, out_ref):
    rows, width = q_ref.shape
    bias = attention_bias(mode, rows, info_ref, lengths_ref, counts_ref, pos_ref)
    lane = lax.broadcasted_iota(jnp.int32, (1, 128), 1)

    def pair(number, carry):
        at = pl.ds(pl.multiple_of(number * 128, 128), 128)
        value_at = pl.ds(pl.multiple_of(number * 128 + width, 128), 128)
        query, keys, values = q_ref[:, at], kv_ref[:, at], kv_ref[:, value_at]
        results = []
        for half in range(2):
            keep = (lane // HEAD_DIM == half).astype(BF16)
            probs = softmax_rows(query * keep, keys, bias)
            results.append(dot(probs.astype(BF16), values))
        out_ref[:, at] = jnp.where(lane < HEAD_DIM, results[0], results[1]).astype(BF16)
        return carry

    lax.fori_loop(0, width // 128, pair, 0)


def attention_backward_body(
    mode, info_ref, lengths_ref, counts_ref, pos_ref, q_ref, kv_ref, g_ref, dq_ref, dkv_ref
):
    rows, width = q_ref.shape
    bias = attention_bias(mode, rows, info_ref, lengths_ref, counts_ref, pos_ref)
    lane = lax.broadcasted_iota(jnp.int32, (1, 128), 1)

    def pair(number, carry):
        at = pl.ds(pl.multiple_of(number * 128, 128), 128)
        value_at = pl.ds(pl.multiple_of(number * 128 + width, 128), 128)
        query, keys, values, grads = q_ref[:, at], kv_ref[:, at], kv_ref[:, value_at], g_ref[:, at]
        d_query, d_keys, d_values = [], [], []
        for half in range(2):
            keep = (lane // HEAD_DIM == half).astype(BF16)
            probs = softmax_rows(query * keep, keys, bias)
            d_probs = dot_nt(grads * keep, values)
            delta = jnp.sum(probs * d_probs, axis=-1, keepdims=True)
            d_scores = (probs * (d_probs - delta)).astype(BF16)
            d_query.append(dot(d_scores, keys) * SCALE)
            d_keys.append(dot_tn(d_scores, query) * SCALE)
            d_values.append(dot_tn(probs.astype(BF16), grads))
        first = lane < HEAD_DIM
        dq_ref[:, at] = jnp.where(first, d_query[0], d_query[1]).astype(BF16)
        dkv_ref[:, at] = jnp.where(first, d_keys[0], d_keys[1]).astype(BF16)
        dkv_ref[:, value_at] = jnp.where(first, d_values[0], d_values[1]).astype(BF16)
        return carry

    lax.fori_loop(0, width // 128, pair, 0)


def smem():
    return pl.BlockSpec(memory_space=pltpu.SMEM)


def vmem():
    return pl.BlockSpec(memory_space=pltpu.VMEM)


def attention_forward(mode, info, lengths, counts, positions, query, kv):
    rows, width = query.shape
    count = kv.shape[0]
    return pl.pallas_call(
        functools.partial(attention_forward_body, mode),
        out_shape=jax.ShapeDtypeStruct((rows, width), BF16),
        in_specs=[smem(), smem(), smem(), vmem(), vmem(), vmem()],
        out_specs=vmem(),
        name=mode + "_forward",
        cost_estimate=pl.CostEstimate(flops=0, bytes_accessed=rows * width, transcendentals=0),
    )(info, lengths, counts, positions, query, kv)


def attention_backward(mode, info, lengths, counts, positions, query, kv, grads):
    rows, width = query.shape
    count = kv.shape[0]
    return pl.pallas_call(
        functools.partial(attention_backward_body, mode),
        out_shape=(jax.ShapeDtypeStruct((rows, width), BF16), jax.ShapeDtypeStruct(kv.shape, BF16)),
        in_specs=[smem(), smem(), smem(), vmem(), vmem(), vmem(), vmem()],
        out_specs=(vmem(), vmem()),
        name=mode + "_backward",
        cost_estimate=pl.CostEstimate(flops=0, bytes_accessed=rows * width, transcendentals=0),
    )(info, lengths, counts, positions, query, kv, grads)


def weight_plan(shards):
    return [(s.shape[0] // 96, s.shape[1]) for s in shards]


def own_body(plan, coords_ref, *refs):
    shards, out, sems = refs[:-2], refs[-2], refs[-1]
    x, c = coords_ref[0], coords_ref[1]
    copies, cursor = [], 0
    for shard, (blocks, width) in zip(shards, plan):
        half = width // 2
        for block in range(blocks):
            row = pl.multiple_of(block * 96 + x * 48, 16)
            column = pl.multiple_of(c * half, 128)
            copies.append(
                pltpu.make_async_copy(
                    shard.at[pl.ds(row, 48), pl.ds(column, half)],
                    out.at[:, pl.ds(cursor, half)],
                    sems.at[len(copies)],
                )
            )
            cursor += half
    for copy in copies:
        copy.start()
    for copy in copies:
        copy.wait()


def own_piece(shards, places):
    plan = weight_plan(shards)
    count = sum(blocks for blocks, _ in plan)
    columns = sum(blocks * width // 2 for blocks, width in plan)
    return pl.pallas_call(
        functools.partial(own_body, plan),
        out_shape=jax.ShapeDtypeStruct((48, columns), BF16),
        in_specs=[smem()] + [pl.BlockSpec(memory_space=pl.ANY)] * len(shards),
        out_specs=vmem(),
        scratch_shapes=[pltpu.SemaphoreType.DMA((count,))],
        name="own_piece",
        cost_estimate=pl.CostEstimate(flops=0, bytes_accessed=48 * columns, transcendentals=0),
    )(places, *shards)


def assemble_copies(plan, straight, coords_ref, arrays, outs, sems, dz):
    x, c, z, y = coords_ref[0], coords_ref[1], coords_ref[2], coords_ref[3]
    copies = []
    per_spot = len(arrays) * sum(blocks for blocks, _ in plan)
    for number, array in enumerate(arrays):
        core = c ^ (number // 4)
        kind = number % 4
        if kind == 0:
            row_x, row_y = x, y
        elif straight:
            row_x, row_y = x ^ (kind // 2), y ^ (kind % 2)
        elif kind == 1:
            row_x, row_y = x ^ (1 - core), y ^ core
        elif kind == 2:
            row_x, row_y = x ^ core, y ^ (1 - core)
        else:
            row_x, row_y = x ^ 1, y ^ 1
        wide = ((z + dz) & (NZ - 1)) * NY + row_y
        cursor = 0
        for out, (blocks, width) in zip(outs, plan):
            half = width // 2
            for block in range(blocks):
                row = pl.multiple_of(wide * (96 * blocks) + block * 96 + row_x * 48, 16)
                column = pl.multiple_of(core * half, 128)
                copies.append(
                    pltpu.make_async_copy(
                        array.at[dz, :, pl.ds(cursor, half)],
                        out.at[pl.ds(row, 48), pl.ds(column, half)],
                        sems.at[dz * per_spot + len(copies)],
                    )
                )
                cursor += half
    return copies


def assemble_body(plan, straight, count, coords_ref, *refs):
    arrays, outs, sems = refs[:count], refs[count:-1], refs[-1]

    def start(dz, carry):
        for copy in assemble_copies(plan, straight, coords_ref, arrays, outs, sems, dz):
            copy.start()
        return carry

    def wait(dz, carry):
        for copy in assemble_copies(plan, straight, coords_ref, arrays, outs, sems, dz):
            copy.wait()
        return carry

    lax.fori_loop(0, NZ, start, 0)
    lax.fori_loop(0, NZ, wait, 0)


def along_line(own, wide):
    return [own] + [move(own, wide, dz=-d) for d in range(1, NZ)]


def tied(*values):
    return lax.optimization_barrier(values)


def assemble(shards, arrays, straight, places, wide):
    plan = weight_plan(shards)
    return pl.pallas_call(
        functools.partial(assemble_body, plan, straight, len(arrays)),
        out_shape=tuple(jax.ShapeDtypeStruct((s.shape[0] * wide, s.shape[1]), BF16) for s in shards),
        in_specs=[smem()] + [pl.BlockSpec(memory_space=pl.ANY)] * len(arrays),
        out_specs=tuple(vmem() for s in shards),
        scratch_shapes=[pltpu.SemaphoreType.DMA((NZ * len(arrays) * sum(blocks for blocks, _ in plan),))],
        name="assemble",
        cost_estimate=pl.CostEstimate(flops=0, bytes_accessed=sum(s.size for s in shards), transcendentals=0),
    )(places, *arrays)


SMALL = 32


def spread_body(places_ref, frames_ref, gains_ref, biases_ref, hidden_ref, out_ref, slab_ref):
    me = places_ref[2] * NY + places_ref[3]
    rows, width = frames_ref.shape
    count = width // gains_ref.shape[1]
    lane = lax.broadcasted_iota(jnp.int32, (1, width), 1)
    mine = (lane >= me * (width // count)) & (lane < (me + 1) * (width // count))
    slab_ref[...] = jnp.zeros((SMALL, width), F32)
    gains = jnp.concatenate([gains_ref[...].astype(F32)] * count, axis=1)
    slab_ref[0:3, :] = jnp.where(mine, gains, 0.0)
    biases = jnp.concatenate([biases_ref[...].astype(F32)] * count, axis=1)
    slab_ref[3:13, :] = jnp.where(mine, biases, 0.0)
    half = hidden_ref.shape[1]
    hidden = jnp.concatenate([hidden_ref[...].astype(F32)] * (width // half), axis=1)
    side = me % NY
    mine = (lane >= side * half) & (lane < (side + 1) * half)
    hidden = jnp.where(mine, hidden, 0.0)
    for row in range(NZ):
        slab_ref[13 + row : 14 + row, :] = jnp.where(me // NY == row, hidden, 0.0)
    out_ref[0:rows, :] = frames_ref[...]
    out_ref[rows : rows + SMALL, :] = slab_ref[...].astype(BF16)


def spread(places, frames, gains, biases, hidden_bias):
    rows, width = frames.shape
    return pl.pallas_call(
        spread_body,
        out_shape=jax.ShapeDtypeStruct((rows + SMALL, width), BF16),
        in_specs=[smem()] + [vmem()] * 4,
        out_specs=vmem(),
        scratch_shapes=[pltpu.VMEM((SMALL, width), F32)],
        name="spread",
        cost_estimate=pl.CostEstimate(flops=0, bytes_accessed=rows * width, transcendentals=0),
    )(places, frames, gains, biases, hidden_bias.reshape(1, -1))


def collect_body(places_ref, *refs):
    lines, tokens, out_ref = refs[:NZ], refs[NZ:-1], refs[-1]
    y = places_ref[3]
    cursor = 0
    for line in lines:
        out_ref[cursor : cursor + line.shape[0], :] = line[...]
        cursor += line.shape[0]
    for first, second in zip(tokens[:-1], tokens[1:]):
        out_ref[cursor : cursor + first.shape[0], :] = jnp.where(y == 0, first[...], second[...])
        cursor += first.shape[0]


def collect(places, lines, tokens):
    rows = sum(v.shape[0] for v in lines) + sum(v.shape[0] for v in tokens[1:])
    width = lines[0].shape[1]
    return pl.pallas_call(
        collect_body,
        out_shape=jax.ShapeDtypeStruct((rows, width), BF16),
        in_specs=[smem()] + [vmem()] * (len(lines) + len(tokens)),
        out_specs=vmem(),
        name="collect",
        cost_estimate=pl.CostEstimate(flops=0, bytes_accessed=rows * width, transcendentals=0),
    )(places, *lines, *tokens)


def prepare_body(*refs):
    lines, tokens, got_ref = refs[:NZ], refs[NZ : NZ + 3], refs[NZ + 3]
    frames_out, normal_out, normed_out, params_out, self_out, cross_out, hidden_out = refs[NZ + 4 :]
    rows = lines[0].shape[0] - SMALL
    width = lines[0].shape[1]
    small = jnp.zeros((SMALL, width), F32)
    for number in range(NZ):
        small = small + lines[number][rows:, :].astype(F32)
        frames_out[number * rows : (number + 1) * rows, :] = lines[number][:rows, :]
    for number in range(NZ):
        at = number * (rows + SMALL)
        small = small + got_ref[at + rows : at + rows + SMALL, :].astype(F32)
        frames_out[(NZ + number) * rows : (NZ + number + 1) * rows, :] = got_ref[at : at + rows, :]
    params_out[...] = small
    self_out[:, :width] = jnp.zeros((1, width), F32)
    self_out[:, width:] = small[7:8, :]
    cross_out[:, :width] = jnp.zeros((1, width), F32)
    cross_out[:, width:] = small[10:11, :]
    for row in range(NZ):
        hidden_out[:, row * width : (row + 1) * width] = small[13 + row : 14 + row, :]
    gain, shift = small[0:1, :], small[3:4, :]
    step = tokens[0].shape[0]
    at = NZ * (rows + SMALL)
    for number in range(5):
        if number < 3:
            block = tokens[number][...]
        else:
            block = got_ref[at + (number - 3) * step : at + (number - 2) * step, :]
        normal = norm_parts(block.astype(F32))[0]
        normal_out[number * step : (number + 1) * step, :] = normal
        normed_out[number * step : (number + 1) * step, :] = (normal * gain + shift).astype(BF16)


def prepare(lines, tokens, got):
    rows = lines[0].shape[0] - SMALL
    step, width = tokens[0].shape
    shapes = [
        ((2 * NZ * rows, width), BF16),
        ((5 * step, width), F32),
        ((5 * step, width), BF16),
        ((SMALL, width), F32),
        ((1, 2 * width), F32),
        ((1, 2 * width), F32),
        ((1, NZ * width), F32),
    ]
    return pl.pallas_call(
        prepare_body,
        out_shape=tuple(jax.ShapeDtypeStruct(shape, dtype) for shape, dtype in shapes),
        in_specs=[vmem()] * (NZ + 4),
        out_specs=tuple(vmem() for _ in shapes),
        name="prepare",
        cost_estimate=pl.CostEstimate(flops=0, bytes_accessed=got.size, transcendentals=0),
    )(*lines, *tokens, got)


def joined(parts):
    return parts[0] if len(parts) == 1 else jnp.concatenate(parts, axis=-1)


def added(kept, arrived):
    return (kept.astype(F32) + arrived.astype(F32)).astype(BF16)


def scatter_steps(pieces, coords, wide):
    x, c, z, y = coords
    views = [p.reshape(NZ, NY, 2, 48, p.shape[-1]) for p in pieces]
    send = joined([jnp.where(c == 0, pick(v, 1 - x, 2), pick(v, 1 - y, 1)) for v in views])
    keep = joined([jnp.where(c == 0, pick(v, x, 2), pick(v, y, 1)) for v in views])
    send, keep = yield send, keep
    arrived = move_mixed(send, wide, 0)
    keep, arrived = yield keep, arrived
    block = added(keep, arrived)
    own = jnp.where(c == 0, y, x)
    send, keep = pick(block, 1 - own, 1), pick(block, own, 1)
    arrived = move_mixed(send, wide, 1)
    keep, arrived = yield keep, arrived
    column = added(keep, arrived)
    column = column.reshape(NZ // 2, 2, *column.shape[1:])
    keep, arrived = yield pick(column, z % 2, 1), flip_z(pick(column, 1 - z % 2, 1), wide, 1)
    pair = added(keep, arrived)
    keep, arrived = yield pick(pair, z // 2, 0), flip_z(pick(pair, 1 - z // 2, 0), wide, 2)
    total = added(keep, arrived)
    other = move(total, wide, dx=1)
    total, other = yield total, other
    mine = jnp.where(x == 0, jnp.concatenate([total, other]), jnp.concatenate([other, total]))
    mine, theirs = yield mine, move(mine, wide, dc=1)
    return mine, theirs


def totals_body(places, *refs):
    out_ref = refs[-1]
    out_ref[...] = jnp.zeros(out_ref.shape, F32)
    width = out_ref.shape[1]
    for (row, start), ref in zip(places, refs[:-1]):
        for number in range((ref.shape[1] - start) // width):
            at = start + number * width
            value = ref[:, at : at + width].astype(F32)
            if ref.shape[0] > 1:
                value = jnp.sum(value, axis=0, keepdims=True)
            out_ref[row + number : row + number + 1, :] = value


def totals(entries, width):
    arrays = [array for _, array, _ in entries]
    return pl.pallas_call(
        functools.partial(totals_body, [(row, start) for row, _, start in entries]),
        out_shape=jax.ShapeDtypeStruct((24, width), F32),
        in_specs=[vmem()] * len(arrays),
        out_specs=vmem(),
        name="totals",
        cost_estimate=pl.CostEstimate(flops=0, bytes_accessed=24 * width, transcendentals=0),
    )(*arrays)


class Chain:
    def __init__(self, steps):
        self.steps = steps
        self.held = next(steps)
        self.result = None

    def finish(self):
        while self.result is None:
            try:
                self.held = self.steps.send(self.held)
            except StopIteration as stop:
                self.result = stop.value
        return self.result


def frame_steps(part, wide):
    arrived = move(part[1], wide, dy=1)
    kept, arrived = yield part[0], arrived
    line = added(kept, arrived)
    arrived = [move(line[d], wide, dz=d) for d in range(1, NZ)]
    total, arrived = yield line[0], arrived
    total = total.astype(F32)
    for value in arrived:
        total = total + value.astype(F32)
    return total


def back_steps(back, y, wide):
    arrived = move(back[3:].astype(BF16), wide, dy=1)
    arrived, back = yield arrived, back
    arrived = arrived.astype(F32)
    line = [
        back[0] + jnp.where(y == 0, arrived[0], 0.0),
        back[1] + jnp.where(y == 0, arrived[1], arrived[0]),
        back[2] + jnp.where(y == 0, 0.0, arrived[1]),
    ]
    arrived = [along_z(line[d].astype(BF16), wide, -d) for d in range(1, 3)]
    own, arrived = yield line[0], arrived
    for value in arrived:
        own = own + value.astype(F32)
    return own


def small_steps(slab, wide):
    moves = (
        lambda v: [move(v, wide, dc=1)],
        lambda v: [move_mixed(v, wide, 0)],
        lambda v: [move_mixed(v, wide, 1)],
        lambda v: [move(v, wide, dz=d) for d in range(1, NZ)],
    )
    for step in moves:
        slab, arrived = yield slab, step(slab)
        for value in arrived:
            slab = slab + value
    return slab


def advance(chains, *values):
    held, values = lax.optimization_barrier(([chain.held for chain in chains], values))
    for chain, kept in zip(chains, held):
        try:
            chain.held = chain.steps.send(kept)
        except StopIteration as stop:
            chain.result = stop.value
    return values[0] if len(values) == 1 else values


def finish_grads(both, shapes, coords):
    c = coords[1]
    mine, theirs = both
    low = jnp.where(c == 0, mine, theirs)
    high = jnp.where(c == 0, theirs, mine)
    shards, cursor = [], 0
    for rows, width in shapes:
        half = width // 2
        blocks = []
        for block in range(rows // 96):
            at = slice(cursor, cursor + half)
            blocks.append(jnp.concatenate([low[:, at], high[:, at]], axis=1))
            cursor += half
        whole = blocks[0] if len(blocks) == 1 else jnp.concatenate(blocks, axis=0)
        shards.append(whole.astype(F32))
    return shards


def per_device(
    tokens,
    frames,
    cotangent,
    item_lengths,
    frame_lengths,
    attn_inputs,
    attn_output,
    cross_queries,
    cross_memory,
    cross_output,
    mlp_inputs,
    mlp_output,
    norm_gains,
    bias_rows,
    mlp_bias,
):
    width = tokens.shape[1]
    tok_rows = tokens.shape[0]
    frame_rows = frames.shape[0]
    hidden_rows = mlp_output.shape[0]
    wide = lax.axis_size("wide")
    me = lax.axis_index("wide").astype(jnp.int32)
    group = lax.axis_index("grp").astype(jnp.int32)
    span = LONGEST // tok_rows
    fast = wide == NZ * NY and span == 4
    x, c, z, y = group // 2, group % 2, me // NY, me % NY
    coords = (x, c, z, y)
    part = width // wide

    self_set = (attn_inputs, attn_output)
    cross_set = (cross_queries, cross_memory, cross_output)
    mlp_set = (mlp_inputs, mlp_output)
    if fast:
        places = jnp.stack(coords).astype(jnp.int32)
        own_self = own_piece(self_set, places)
        self_parts = along_line(own_self, wide)
        line = spread(places, frames, norm_gains, bias_rows, mlp_bias)
        own_cross = own_piece(cross_set, places)
        own_mlp = own_piece(mlp_set, places)
        self_parts, line, own_tokens, own_cross, own_mlp = tied(self_parts, line, tokens, own_cross, own_mlp)
        self_parts = [jnp.stack(self_parts)]
        self_parts += [move(self_parts[0], wide, dy=1), move(self_parts[0], wide, dx=1)]
        lines = [line] + [move(line, wide, dz=-d) for d in range(1, NZ)]
        blocks_mine = [own_tokens, along_z(own_tokens, wide, 1), along_z(own_tokens, wide, 2)]
        payload = collect(places, lines, blocks_mine)
        payload, self_parts, own_cross, own_mlp = tied(payload, self_parts, own_cross, own_mlp)
        got = move(payload, wide, dy=1)
        self_parts.append(move(self_parts[1], wide, dx=1))
        self_theirs = [move(v, wide, dc=1) for v in self_parts[:3]]
        cross_parts = along_line(own_cross, wide)
        cross_parts, self_parts, own_mlp = tied(cross_parts, self_parts, own_mlp)
        cross_parts = [jnp.stack(cross_parts)]
        cross_parts += [move(cross_parts[0], wide, dy=1), move(cross_parts[0], wide, dx=1)]
        self_theirs.append(move(self_parts[3], wide, dc=1))
        mlp_parts = along_line(own_mlp, wide)
        all_frames, normal_window, normed_window, params, self_bias, cross_bias, hidden_bias = prepare(
            lines, blocks_mine, got
        )
        w_in, w_out = assemble(self_set, self_parts + self_theirs, True, places, wide)
        cross_parts, w_in, normed_window = tied(cross_parts, w_in, normed_window)
        cross_parts.append(move(cross_parts[1], wide, dx=1))
        cross_theirs = [move(v, wide, dc=1) for v in cross_parts[:3]]
        gains, biases = params[:3], params[3:13]
        number = jnp.arange(wide, dtype=jnp.int32)
        owner = ((z + number % NZ) % NZ) * NY + (y ^ (number // NZ))
        blocks_at = me - jnp.array([0, 2, 4, 1, 3], jnp.int32)
    else:
        gather = functools.partial(lax.all_gather, axis_name="wide", axis=0, tiled=True)
        window = jnp.concatenate([tokens] + [shifted(tokens, wide, o) for o in range(1, span + 1)])
        blocks_at = me - jnp.arange(span + 1, dtype=jnp.int32)
        all_frames = gather(frames)
        owner = jnp.arange(wide, dtype=jnp.int32)
        small = jnp.concatenate([norm_gains.reshape(-1), bias_rows.reshape(-1), mlp_bias])
        params = gather(small.reshape(1, -1))
        w_in, w_out, w_cross_q, w_memory, w_cross_out = [gather(v) for v in self_set + cross_set]
        w_mlp_in, w_mlp_out = [gather(v) for v in mlp_set]
        gains = params[:, : 3 * part].reshape(wide, 3, part).transpose(1, 0, 2).reshape(3, width).astype(F32)
        biases = params[:, 3 * part : 13 * part].reshape(wide, 10, part).transpose(1, 0, 2)
        biases = biases.reshape(10, width).astype(F32)
        hidden_bias = params[:, 13 * part : 13 * part + hidden_rows].reshape(1, -1).astype(F32)
        zero_row = jnp.zeros((1, width), F32)
        self_bias = jnp.concatenate([zero_row, biases[4:5]], axis=1)
        cross_bias = jnp.concatenate([zero_row, biases[7:8]], axis=1)
        normal_window = norm_parts(window.astype(F32))[0]
        normed_window = (normal_window * gains[:1] + biases[:1]).astype(BF16)
    frame_pos = (owner[:, None] * frame_rows + jnp.arange(frame_rows, dtype=jnp.int32)).reshape(1, -1)
    key_pos = (blocks_at[:, None] * tok_rows + jnp.arange(tok_rows, dtype=jnp.int32)).reshape(1, -1)

    def gain(row):
        return gains[row : row + 1]

    def bias(row):
        return biases[row : row + 1]

    info = me.reshape(1)

    def swapped(parts):
        theirs = move(jnp.concatenate(parts), wide, dc=1)
        found, cursor = [], 0
        for value in parts:
            found.append(theirs[cursor : cursor + value.shape[0]])
            cursor += value.shape[0]
        return found

    def halves(values):
        half = values[0].shape[1] // 2
        mine = [lax.dynamic_slice_in_dim(v, c * half, half, 1) for v in values]
        theirs = swapped([lax.dynamic_slice_in_dim(v, (1 - c) * half, half, 1) for v in values])
        return [jnp.concatenate(pair) for pair in zip(mine, theirs)]

    def doubled(values):
        return [jnp.concatenate(pair) for pair in zip(values, swapped(values))]

    def weight(left, right):
        grad = dot_tn(left, right).astype(BF16)
        return grad.reshape(wide, -1, 96, grad.shape[1])

    def blocks(*grads):
        return [grad[:, i] for grad in grads for i in range(grad.shape[1])]

    inputs = tokens.astype(F32)
    normed_one = normed_window[:tok_rows]
    query = (dot(normed_one, w_in[:, :width]) + bias(3)).astype(BF16)
    self_kv = (dot(normed_window, w_in[:, width:]) + self_bias).astype(BF16)
    tables = (info, item_lengths, frame_lengths)
    if fast:
        cross_parts, mlp_parts, self_kv = tied(cross_parts, mlp_parts, self_kv)
        cross_theirs.append(move(cross_parts[3], wide, dc=1))
        mlp_parts = [jnp.stack(mlp_parts)]
        mlp_parts += [move_mixed(mlp_parts[0], wide, 0), move_mixed(mlp_parts[0], wide, 1)]
        w_cross_q, w_memory, w_cross_out = assemble(cross_set, cross_parts + cross_theirs, True, places, wide)
    attended = attention_forward("self", *tables, key_pos, query, self_kv)
    after_one = inputs + dot(attended, w_out) + bias(5)
    normed_two = norm_apply(after_one, gain(1), bias(1)).astype(BF16)
    cross_q = (dot(normed_two, w_cross_q) + bias(6)).astype(BF16)
    memory = (dot(all_frames, w_memory) + cross_bias).astype(BF16)
    if fast:
        mlp_parts, memory = tied(mlp_parts, memory)
        mlp_parts.append(move_mixed(mlp_parts[1], wide, 1))
        mlp_theirs = [move(v, wide, dc=1) for v in mlp_parts[:3]]
    cross_att = attention_forward("cross", *tables, frame_pos, cross_q, memory)
    if fast:
        mlp_theirs.append(move(mlp_parts[3], wide, dc=1))
        w_mlp_in, w_mlp_out = assemble(mlp_set, mlp_parts + mlp_theirs, False, places, wide)
    after_two = after_one + dot(cross_att, w_cross_out) + bias(8)
    normed_three = norm_apply(after_two, gain(2), bias(2)).astype(BF16)
    pre_act = dot(normed_three, w_mlp_in) + hidden_bias
    exact_gelu = functools.partial(jax.nn.gelu, approximate=False)
    hidden = exact_gelu(pre_act).astype(BF16)

    grad_out = cotangent.astype(F32)
    grad_hidden = dot_nt(cotangent, w_mlp_out)
    grad_pre = jax.vjp(exact_gelu, pre_act)[1](grad_hidden)[0].astype(BF16)
    if fast:
        window_two, frames_two, attended_two, two_two, cross_att_two, three_two = doubled(
            [normed_window, all_frames, attended, normed_two, cross_att, normed_three]
        )
        rows_two = normed_window.shape[0]
        one_two = jnp.concatenate([window_two[:tok_rows], window_two[rows_two : rows_two + tok_rows]])
        (hidden_two,) = doubled([hidden])
        (out_half,) = halves([cotangent])
        chain_out = Chain(scatter_steps(blocks(weight(hidden_two, out_half)), coords, wide))
        grad_pre = advance([chain_out], grad_pre)
        (pre_half,) = halves([grad_pre])
        chain_in = Chain(scatter_steps(blocks(weight(three_two, pre_half)), coords, wide))
        grad_pre = advance([chain_in], grad_pre)
    grad_three, gain_three, shift_three = norm_back(after_two, gain(2), dot_nt(grad_pre, w_mlp_in))
    grad_after_two = grad_out + grad_three
    grad_cross_branch = grad_after_two.astype(BF16)
    grad_cross_att = dot_nt(grad_cross_branch, w_cross_out).astype(BF16)
    grad_cross_q, grad_memory = attention_backward(
        "cross", *tables, frame_pos, cross_q, memory, grad_cross_att
    )
    if fast:
        grad_cross_q, grad_memory = advance([chain_out], grad_cross_q, grad_memory)
    grad_two, gain_two, shift_two = norm_back(after_one, gain(1), dot_nt(grad_cross_q, w_cross_q))
    grad_after_one = grad_after_two + grad_two
    grad_self_branch = grad_after_one.astype(BF16)
    if fast:
        grad_self_branch = advance([chain_in], grad_self_branch)
    grad_attended = dot_nt(grad_self_branch, w_out).astype(BF16)

    frame_part = dot_nt(grad_memory, w_memory)
    if fast:
        branch_half, cross_half, keys_half, values_half, self_half = halves(
            [grad_cross_branch, grad_cross_q, grad_memory[:, :width], grad_memory[:, width:], grad_self_branch]
        )
        pieces = blocks(
            weight(frames_two, keys_half),
            weight(frames_two, values_half),
            weight(cross_att_two, branch_half),
            weight(two_two, cross_half),
            weight(attended_two, self_half),
        )
        chain_cross = Chain(scatter_steps(pieces, coords, wide))
        frame_part = frame_part.astype(BF16).reshape(NY, NZ, frame_rows, width)
        chain_frames = Chain(frame_steps(frame_part, wide))
        grad_attended = advance([chain_out, chain_cross], grad_attended)
    else:
        grad_frames = lax.psum_scatter(frame_part, "wide", scatter_dimension=0, tiled=True)
    grad_query, grad_kv = attention_backward("self", *tables, key_pos, query, self_kv, grad_attended)
    if fast:
        grad_query, grad_kv = advance([chain_cross, chain_out], grad_query, grad_kv)
        query_half, keys_half, values_half = halves([grad_query, grad_kv[:, :width], grad_kv[:, width:]])
        grad_in = [weight(one_two, query_half), weight(window_two, keys_half), weight(window_two, values_half)]
        chain_self = Chain(scatter_steps(blocks(*grad_in), coords, wide))
        grad_kv, grad_pre, hidden = advance(
            [chain_self, chain_in, chain_out, chain_frames], grad_kv, grad_pre, hidden
        )

    window_part = dot_nt(grad_kv, w_in[:, width:])
    own_part = window_part[:tok_rows] + dot_nt(grad_query, w_in[:, :width])
    window_part = jnp.concatenate([own_part, window_part[tok_rows:]])
    gain_one = jnp.sum(window_part * normal_window, axis=0, keepdims=True)
    shift_one = jnp.sum(window_part, axis=0, keepdims=True)
    last_gain = gain(0)
    if fast:
        back = window_part.reshape(5, tok_rows, width)
        chain_back = Chain(back_steps(back, y, wide))
        rows = [
            (0, gain_one, 0),
            (1, gain_two, 0),
            (2, gain_three, 0),
            (3, shift_one, 0),
            (4, shift_two, 0),
            (5, shift_three, 0),
            (6, grad_query, 0),
            (7, grad_kv, width),
            (8, grad_self_branch, 0),
            (9, grad_cross_q, 0),
            (10, grad_memory, width),
            (11, grad_cross_branch, 0),
            (12, cotangent, 0),
            (13, grad_pre, 0),
        ]
        chain_small = Chain(small_steps(totals(rows, width), wide))
        last_gain, hidden = advance([chain_self, chain_cross, chain_in, chain_small], last_gain, hidden)
        last_gain = advance([chain_self, chain_cross, chain_in, chain_back, chain_small, chain_out], last_gain)
        last_gain = advance([chain_self, chain_cross, chain_small, chain_in, chain_frames], last_gain)
        last_gain = advance([chain_self, chain_cross, chain_small], last_gain)
        last_gain = advance([chain_self, chain_back], last_gain)
        grad_one = chain_back.finish()
        grad_frames = chain_frames.finish()
        small = chain_small.finish()
    else:
        grad_one = own_part
        for o in range(1, span + 1):
            block = window_part[o * tok_rows : (o + 1) * tok_rows]
            grad_one = grad_one + shifted(block.astype(BF16), wide, -o).astype(F32)
    block_output = (after_two + dot(hidden, w_mlp_out) + bias(9)).astype(BF16)
    grad_tokens = grad_after_one + norm_back(inputs, last_gain, grad_one)[0]

    if fast:
        small_hidden = pick(small[13:17], me // NY, 0)
        small_hidden = lax.dynamic_slice_in_dim(small_hidden, (me % NY) * hidden_rows, hidden_rows, 0)
        small = lax.dynamic_slice_in_dim(small, me * part, part, 1)
        square = (part, width)
        (g_mlp_in,) = finish_grads(chain_in.finish(), [mlp_inputs.shape], coords)
        (g_mlp_out,) = finish_grads(chain_out.finish(), [mlp_output.shape], coords)
        g_memory_k, g_memory_v, g_cross_out, g_cross_q, g_out = finish_grads(
            chain_cross.finish(), [square] * 5, coords
        )
        g_in_q, g_in_k, g_in_v = finish_grads(chain_self.finish(), [square] * 3, coords)
        g_memory = jnp.concatenate([g_memory_k, g_memory_v], axis=1)
        g_in = jnp.concatenate([g_in_q, g_in_k, g_in_v], axis=1)
        rows_all, g_bias = small[:13], small_hidden
    else:

        def weight_sum(left, right):
            grad = lax.psum_scatter(dot_tn(left, right), "wide", scatter_dimension=0, tiled=True)
            return lax.psum(grad.astype(BF16), "grp").astype(F32)

        def total(value):
            return jnp.sum(value.astype(F32), axis=0, keepdims=True)

        rows = [
            gain_one,
            gain_two,
            gain_three,
            shift_one,
            shift_two,
            shift_three,
            total(grad_query),
            total(grad_kv[:, width:]),
            total(grad_self_branch),
            total(grad_cross_q),
            total(grad_memory[:, width:]),
            total(grad_cross_branch),
            total(grad_out),
        ]
        g_in = jnp.concatenate(
            [weight_sum(normed_one, grad_query), weight_sum(normed_window, grad_kv)], axis=1
        )
        g_out = weight_sum(attended, grad_self_branch)
        g_cross_q = weight_sum(normed_two, grad_cross_q)
        g_memory = weight_sum(all_frames, grad_memory)
        g_cross_out = weight_sum(cross_att, grad_cross_branch)
        g_mlp_in = weight_sum(normed_three, grad_pre)
        g_mlp_out = weight_sum(hidden, cotangent)
        small = lax.psum(jnp.concatenate(rows), BOTH)
        rows_all = lax.dynamic_slice_in_dim(small, me * part, part, 1)
        g_bias = lax.psum(total(grad_pre).reshape(-1), BOTH)
        g_bias = lax.dynamic_slice_in_dim(g_bias, me * hidden_rows, hidden_rows, 0)
    return (
        block_output,
        grad_tokens,
        grad_frames,
        g_in,
        g_out,
        g_cross_q,
        g_memory,
        g_cross_out,
        g_mlp_in,
        g_mlp_out,
        rows_all[:3],
        rows_all[3:],
        g_bias,
    )


def solution(mesh):
    rows = P(BOTH, None)
    weight = P("wide", None)
    columns = P(None, "wide")
    return jax.shard_map(
        per_device,
        mesh=mesh,
        in_specs=(rows,) * 3 + (P("grp", None),) * 2 + (weight,) * 7 + (columns, columns, P("wide")),
        out_specs=(rows,) * 3 + (weight,) * 7 + (columns, columns, P("wide")),
        check_vma=False,
    )
```

```python
import functools

import jax
import jax.numpy as jnp
from jax import lax
from jax.experimental import pallas as pl
from jax.experimental.pallas import tpu as pltpu
from jax.sharding import PartitionSpec as P

HEADS = 12
HEAD_DIM = 64
LONGEST = 512
EPSILON = 1e-05
MASKED = -1e30
SCALE = HEAD_DIM ** (-0.5)
F32 = jnp.float32
BF16 = jnp.bfloat16
BOTH = ("grp", "wide")
NZ, NY = 4, 2


def dot(left, right):
    return jnp.dot(left, right, preferred_element_type=F32)


def dot_tn(left, right):
    return lax.dot_general(left, right, (((0,), (0,)), ((), ())), preferred_element_type=F32)


def dot_nt(left, right):
    return lax.dot_general(left, right, (((1,), (1,)), ((), ())), preferred_element_type=F32)


def norm_parts(values):
    centre = jnp.mean(values, axis=-1, keepdims=True)
    centred = values - centre
    spread = jnp.mean(centred * centred, axis=-1, keepdims=True)
    inverse = lax.rsqrt(spread + EPSILON)
    return centred * inverse, inverse


def norm_apply(values, gain, shift):
    return norm_parts(values)[0] * gain + shift


def norm_back(values, gain, upstream):
    normal, inverse = norm_parts(values)
    scaled = upstream * gain
    mean_one = jnp.mean(scaled, axis=-1, keepdims=True)
    mean_two = jnp.mean(scaled * normal, axis=-1, keepdims=True)
    grad = inverse * (scaled - mean_one - normal * mean_two)
    return grad, jnp.sum(upstream * normal, axis=0, keepdims=True), jnp.sum(upstream, axis=0, keepdims=True)


def move(value, wide, dx=0, dc=0, dz=0, dy=0):
    pairs = []
    for x in range(2):
        for c in range(2):
            for z in range(NZ):
                for y in range(NY):
                    source = (x * 2 + c) * wide + z * NY + y
                    target = ((x ^ dx) * 2 + (c ^ dc)) * wide + ((z + dz) % NZ) * NY + (y ^ dy)
                    pairs.append((source, target))
    return lax.ppermute(value, BOTH, pairs)


def move_mixed(value, wide, turn):
    pairs = []
    for x in range(2):
        for c in range(2):
            dx = int(c == turn)
            for z in range(NZ):
                for y in range(NY):
                    source = (x * 2 + c) * wide + z * NY + y
                    target = ((x ^ dx) * 2 + c) * wide + z * NY + (y ^ 1 ^ dx)
                    pairs.append((source, target))
    return lax.ppermute(value, BOTH, pairs)


def shifted(value, wide, by):
    pairs = [(i, i + by) for i in range(wide) if 0 <= i + by < wide]
    return lax.ppermute(value, "wide", pairs)


def along_z(value, wide, by):
    pairs = []
    for group in range(4):
        for z in range(NZ):
            for y in range(NY):
                if 0 <= z + by < NZ:
                    source = group * wide + z * NY + y
                    pairs.append((source, source + by * NY))
    return lax.ppermute(value, BOTH, pairs)


def flip_z(value, wide, bit):
    pairs = []
    for group in range(4):
        for z in range(NZ):
            for y in range(NY):
                pairs.append((group * wide + z * NY + y, group * wide + (z ^ bit) * NY + y))
    return lax.ppermute(value, BOTH, pairs)


def pick(value, index, axis):
    return lax.dynamic_index_in_dim(value, index, axis, keepdims=False)


def attention_bias(mode, tok_rows, info_ref, lengths_ref, counts_ref, pos_ref):
    items = lengths_ref.shape[1]
    slot = info_ref[0] * tok_rows + lax.broadcasted_iota(jnp.int32, (tok_rows, 1), 0)
    key = pos_ref[...]
    if mode == "self":
        first = jnp.zeros((tok_rows, 1), jnp.int32)
        start = jnp.int32(0)
        for item in range(items):
            first = jnp.where(slot >= start, start, first)
            start = start + lengths_ref[0, item]
        allowed = (key >= first) & (key <= slot)
    else:
        owner = jnp.zeros((tok_rows, 1), jnp.int32)
        frame_owner = jnp.zeros(key.shape, jnp.int32)
        end = jnp.int32(0)
        frame_end = jnp.int32(0)
        for item in range(items):
            end = end + lengths_ref[0, item]
            frame_end = frame_end + counts_ref[0, item]
            owner = owner + (slot >= end).astype(jnp.int32)
            frame_owner = frame_owner + (key >= frame_end).astype(jnp.int32)
        allowed = owner == frame_owner
    return jnp.where(allowed, 0.0, MASKED).astype(F32)


def softmax_rows(query, keys, bias):
    scores = dot_nt(query, keys) * SCALE + bias
    top = jnp.max(scores, axis=-1, keepdims=True)
    raised = jnp.exp(scores - top)
    return raised / jnp.sum(raised, axis=-1, keepdims=True)


def attention_forward_body(mode, info_ref, lengths_ref, counts_ref, pos_ref, q_ref, kv_ref, out_ref):
    rows, width = q_ref.shape
    bias = attention_bias(mode, rows, info_ref, lengths_ref, counts_ref, pos_ref)
    lane = lax.broadcasted_iota(jnp.int32, (1, 128), 1)

    def pair(number, carry):
        at = pl.ds(pl.multiple_of(number * 128, 128), 128)
        value_at = pl.ds(pl.multiple_of(number * 128 + width, 128), 128)
        query, keys, values = q_ref[:, at], kv_ref[:, at], kv_ref[:, value_at]
        results = []
        for half in range(2):
            keep = (lane // HEAD_DIM == half).astype(BF16)
            probs = softmax_rows(query * keep, keys, bias)
            results.append(dot(probs.astype(BF16), values))
        out_ref[:, at] = jnp.where(lane < HEAD_DIM, results[0], results[1]).astype(BF16)
        return carry

    lax.fori_loop(0, width // 128, pair, 0)


def attention_backward_body(
    mode, info_ref, lengths_ref, counts_ref, pos_ref, q_ref, kv_ref, g_ref, dq_ref, dkv_ref
):
    rows, width = q_ref.shape
    bias = attention_bias(mode, rows, info_ref, lengths_ref, counts_ref, pos_ref)
    lane = lax.broadcasted_iota(jnp.int32, (1, 128), 1)

    def pair(number, carry):
        at = pl.ds(pl.multiple_of(number * 128, 128), 128)
        value_at = pl.ds(pl.multiple_of(number * 128 + width, 128), 128)
        query, keys, values, grads = q_ref[:, at], kv_ref[:, at], kv_ref[:, value_at], g_ref[:, at]
        d_query, d_keys, d_values = [], [], []
        for half in range(2):
            keep = (lane // HEAD_DIM == half).astype(BF16)
            probs = softmax_rows(query * keep, keys, bias)
            d_probs = dot_nt(grads * keep, values)
            delta = jnp.sum(probs * d_probs, axis=-1, keepdims=True)
            d_scores = (probs * (d_probs - delta)).astype(BF16)
            d_query.append(dot(d_scores, keys) * SCALE)
            d_keys.append(dot_tn(d_scores, query) * SCALE)
            d_values.append(dot_tn(probs.astype(BF16), grads))
        first = lane < HEAD_DIM
        dq_ref[:, at] = jnp.where(first, d_query[0], d_query[1]).astype(BF16)
        dkv_ref[:, at] = jnp.where(first, d_keys[0], d_keys[1]).astype(BF16)
        dkv_ref[:, value_at] = jnp.where(first, d_values[0], d_values[1]).astype(BF16)
        return carry

    lax.fori_loop(0, width // 128, pair, 0)


def smem():
    return pl.BlockSpec(memory_space=pltpu.SMEM)


def vmem():
    return pl.BlockSpec(memory_space=pltpu.VMEM)


def attention_forward(mode, info, lengths, counts, positions, query, kv):
    rows, width = query.shape
    count = kv.shape[0]
    return pl.pallas_call(
        functools.partial(attention_forward_body, mode),
        out_shape=jax.ShapeDtypeStruct((rows, width), BF16),
        in_specs=[smem(), smem(), smem(), vmem(), vmem(), vmem()],
        out_specs=vmem(),
        name=mode + "_forward",
        cost_estimate=pl.CostEstimate(flops=0, bytes_accessed=rows * width, transcendentals=0),
    )(info, lengths, counts, positions, query, kv)


def attention_backward(mode, info, lengths, counts, positions, query, kv, grads):
    rows, width = query.shape
    count = kv.shape[0]
    return pl.pallas_call(
        functools.partial(attention_backward_body, mode),
        out_shape=(jax.ShapeDtypeStruct((rows, width), BF16), jax.ShapeDtypeStruct(kv.shape, BF16)),
        in_specs=[smem(), smem(), smem(), vmem(), vmem(), vmem(), vmem()],
        out_specs=(vmem(), vmem()),
        name=mode + "_backward",
        cost_estimate=pl.CostEstimate(flops=0, bytes_accessed=rows * width, transcendentals=0),
    )(info, lengths, counts, positions, query, kv, grads)


def weight_plan(shards):
    return [(s.shape[0] // 96, s.shape[1]) for s in shards]


def own_body(plan, coords_ref, *refs):
    shards, out, sems = refs[:-2], refs[-2], refs[-1]
    x, c = coords_ref[0], coords_ref[1]
    copies, cursor = [], 0
    for shard, (blocks, width) in zip(shards, plan):
        half = width // 2
        for block in range(blocks):
            row = pl.multiple_of(block * 96 + x * 48, 16)
            column = pl.multiple_of(c * half, 128)
            copies.append(
                pltpu.make_async_copy(
                    shard.at[pl.ds(row, 48), pl.ds(column, half)],
                    out.at[:, pl.ds(cursor, half)],
                    sems.at[len(copies)],
                )
            )
            cursor += half
    for copy in copies:
        copy.start()
    for copy in copies:
        copy.wait()


def own_piece(shards, places):
    plan = weight_plan(shards)
    count = sum(blocks for blocks, _ in plan)
    columns = sum(blocks * width // 2 for blocks, width in plan)
    return pl.pallas_call(
        functools.partial(own_body, plan),
        out_shape=jax.ShapeDtypeStruct((48, columns), BF16),
        in_specs=[smem()] + [pl.BlockSpec(memory_space=pl.ANY)] * len(shards),
        out_specs=vmem(),
        scratch_shapes=[pltpu.SemaphoreType.DMA((count,))],
        name="own_piece",
        cost_estimate=pl.CostEstimate(flops=0, bytes_accessed=48 * columns, transcendentals=0),
    )(places, *shards)


def assemble_copies(plan, straight, coords_ref, arrays, outs, sems, dz):
    x, c, z, y = coords_ref[0], coords_ref[1], coords_ref[2], coords_ref[3]
    copies = []
    per_spot = len(arrays) * sum(blocks for blocks, _ in plan)
    for number, array in enumerate(arrays):
        core = c ^ (number // 4)
        kind = number % 4
        if kind == 0:
            row_x, row_y = x, y
        elif straight:
            row_x, row_y = x ^ (kind // 2), y ^ (kind % 2)
        elif kind == 1:
            row_x, row_y = x ^ (1 - core), y ^ core
        elif kind == 2:
            row_x, row_y = x ^ core, y ^ (1 - core)
        else:
            row_x, row_y = x ^ 1, y ^ 1
        wide = ((z + dz) & (NZ - 1)) * NY + row_y
        cursor = 0
        for out, (blocks, width) in zip(outs, plan):
            half = width // 2
            for block in range(blocks):
                row = pl.multiple_of(wide * (96 * blocks) + block * 96 + row_x * 48, 16)
                column = pl.multiple_of(core * half, 128)
                copies.append(
                    pltpu.make_async_copy(
                        array.at[dz, :, pl.ds(cursor, half)],
                        out.at[pl.ds(row, 48), pl.ds(column, half)],
                        sems.at[dz * per_spot + len(copies)],
                    )
                )
                cursor += half
    return copies


def assemble_body(plan, straight, count, coords_ref, *refs):
    arrays, outs, sems = refs[:count], refs[count:-1], refs[-1]

    def start(dz, carry):
        for copy in assemble_copies(plan, straight, coords_ref, arrays, outs, sems, dz):
            copy.start()
        return carry

    def wait(dz, carry):
        for copy in assemble_copies(plan, straight, coords_ref, arrays, outs, sems, dz):
            copy.wait()
        return carry

    lax.fori_loop(0, NZ, start, 0)
    lax.fori_loop(0, NZ, wait, 0)


def along_line(own, wide):
    return [own] + [move(own, wide, dz=-d) for d in range(1, NZ)]


def tied(*values):
    return lax.optimization_barrier(values)


def assemble(shards, arrays, straight, places, wide):
    plan = weight_plan(shards)
    return pl.pallas_call(
        functools.partial(assemble_body, plan, straight, len(arrays)),
        out_shape=tuple(jax.ShapeDtypeStruct((s.shape[0] * wide, s.shape[1]), BF16) for s in shards),
        in_specs=[smem()] + [pl.BlockSpec(memory_space=pl.ANY)] * len(arrays),
        out_specs=tuple(vmem() for s in shards),
        scratch_shapes=[pltpu.SemaphoreType.DMA((NZ * len(arrays) * sum(blocks for blocks, _ in plan),))],
        name="assemble",
        cost_estimate=pl.CostEstimate(flops=0, bytes_accessed=sum(s.size for s in shards), transcendentals=0),
    )(places, *arrays)


SMALL = 32


def spread_body(places_ref, frames_ref, gains_ref, biases_ref, hidden_ref, out_ref, slab_ref):
    me = places_ref[2] * NY + places_ref[3]
    rows, width = frames_ref.shape
    count = width // gains_ref.shape[1]
    lane = lax.broadcasted_iota(jnp.int32, (1, width), 1)
    mine = (lane >= me * (width // count)) & (lane < (me + 1) * (width // count))
    slab_ref[...] = jnp.zeros((SMALL, width), F32)
    gains = jnp.concatenate([gains_ref[...].astype(F32)] * count, axis=1)
    slab_ref[0:3, :] = jnp.where(mine, gains, 0.0)
    biases = jnp.concatenate([biases_ref[...].astype(F32)] * count, axis=1)
    slab_ref[3:13, :] = jnp.where(mine, biases, 0.0)
    half = hidden_ref.shape[1]
    hidden = jnp.concatenate([hidden_ref[...].astype(F32)] * (width // half), axis=1)
    side = me % NY
    mine = (lane >= side * half) & (lane < (side + 1) * half)
    hidden = jnp.where(mine, hidden, 0.0)
    for row in range(NZ):
        slab_ref[13 + row : 14 + row, :] = jnp.where(me // NY == row, hidden, 0.0)
    out_ref[0:rows, :] = frames_ref[...]
    out_ref[rows : rows + SMALL, :] = slab_ref[...].astype(BF16)


def spread(places, frames, gains, biases, hidden_bias):
    rows, width = frames.shape
    return pl.pallas_call(
        spread_body,
        out_shape=jax.ShapeDtypeStruct((rows + SMALL, width), BF16),
        in_specs=[smem()] + [vmem()] * 4,
        out_specs=vmem(),
        scratch_shapes=[pltpu.VMEM((SMALL, width), F32)],
        name="spread",
        cost_estimate=pl.CostEstimate(flops=0, bytes_accessed=rows * width, transcendentals=0),
    )(places, frames, gains, biases, hidden_bias.reshape(1, -1))


def collect_body(places_ref, *refs):
    lines, tokens, out_ref = refs[:NZ], refs[NZ:-1], refs[-1]
    y = places_ref[3]
    cursor = 0
    for line in lines:
        out_ref[cursor : cursor + line.shape[0], :] = line[...]
        cursor += line.shape[0]
    for first, second in zip(tokens[:-1], tokens[1:]):
        out_ref[cursor : cursor + first.shape[0], :] = jnp.where(y == 0, first[...], second[...])
        cursor += first.shape[0]


def collect(places, lines, tokens):
    rows = sum(v.shape[0] for v in lines) + sum(v.shape[0] for v in tokens[1:])
    width = lines[0].shape[1]
    return pl.pallas_call(
        collect_body,
        out_shape=jax.ShapeDtypeStruct((rows, width), BF16),
        in_specs=[smem()] + [vmem()] * (len(lines) + len(tokens)),
        out_specs=vmem(),
        name="collect",
        cost_estimate=pl.CostEstimate(flops=0, bytes_accessed=rows * width, transcendentals=0),
    )(places, *lines, *tokens)


def prepare_body(*refs):
    lines, tokens, got_ref = refs[:NZ], refs[NZ : NZ + 3], refs[NZ + 3]
    frames_out, normal_out, normed_out, params_out, self_out, cross_out, hidden_out = refs[NZ + 4 :]
    rows = lines[0].shape[0] - SMALL
    width = lines[0].shape[1]
    small = jnp.zeros((SMALL, width), F32)
    for number in range(NZ):
        small = small + lines[number][rows:, :].astype(F32)
        frames_out[number * rows : (number + 1) * rows, :] = lines[number][:rows, :]
    for number in range(NZ):
        at = number * (rows + SMALL)
        small = small + got_ref[at + rows : at + rows + SMALL, :].astype(F32)
        frames_out[(NZ + number) * rows : (NZ + number + 1) * rows, :] = got_ref[at : at + rows, :]
    params_out[...] = small
    self_out[:, :width] = jnp.zeros((1, width), F32)
    self_out[:, width:] = small[7:8, :]
    cross_out[:, :width] = jnp.zeros((1, width), F32)
    cross_out[:, width:] = small[10:11, :]
    for row in range(NZ):
        hidden_out[:, row * width : (row + 1) * width] = small[13 + row : 14 + row, :]
    gain, shift = small[0:1, :], small[3:4, :]
    step = tokens[0].shape[0]
    at = NZ * (rows + SMALL)
    for number in range(5):
        if number < 3:
            block = tokens[number][...]
        else:
            block = got_ref[at + (number - 3) * step : at + (number - 2) * step, :]
        normal = norm_parts(block.astype(F32))[0]
        normal_out[number * step : (number + 1) * step, :] = normal
        normed_out[number * step : (number + 1) * step, :] = (normal * gain + shift).astype(BF16)


def prepare(lines, tokens, got):
    rows = lines[0].shape[0] - SMALL
    step, width = tokens[0].shape
    shapes = [
        ((2 * NZ * rows, width), BF16),
        ((5 * step, width), F32),
        ((5 * step, width), BF16),
        ((SMALL, width), F32),
        ((1, 2 * width), F32),
        ((1, 2 * width), F32),
        ((1, NZ * width), F32),
    ]
    return pl.pallas_call(
        prepare_body,
        out_shape=tuple(jax.ShapeDtypeStruct(shape, dtype) for shape, dtype in shapes),
        in_specs=[vmem()] * (NZ + 4),
        out_specs=tuple(vmem() for _ in shapes),
        name="prepare",
        cost_estimate=pl.CostEstimate(flops=0, bytes_accessed=got.size, transcendentals=0),
    )(*lines, *tokens, got)


def joined(parts):
    return parts[0] if len(parts) == 1 else jnp.concatenate(parts, axis=-1)


def added(kept, arrived):
    return (kept.astype(F32) + arrived.astype(F32)).astype(BF16)


def scatter_steps(pieces, coords, wide):
    x, c, z, y = coords
    views = [p.reshape(NZ, NY, 2, 48, p.shape[-1]) for p in pieces]
    send = joined([jnp.where(c == 0, pick(v, 1 - x, 2), pick(v, 1 - y, 1)) for v in views])
    keep = joined([jnp.where(c == 0, pick(v, x, 2), pick(v, y, 1)) for v in views])
    send, keep = yield send, keep
    arrived = move_mixed(send, wide, 0)
    keep, arrived = yield keep, arrived
    block = added(keep, arrived)
    own = jnp.where(c == 0, y, x)
    send, keep = pick(block, 1 - own, 1), pick(block, own, 1)
    arrived = move_mixed(send, wide, 1)
    keep, arrived = yield keep, arrived
    column = added(keep, arrived)
    column = column.reshape(NZ // 2, 2, *column.shape[1:])
    keep, arrived = yield pick(column, z % 2, 1), flip_z(pick(column, 1 - z % 2, 1), wide, 1)
    pair = added(keep, arrived)
    keep, arrived = yield pick(pair, z // 2, 0), flip_z(pick(pair, 1 - z // 2, 0), wide, 2)
    total = added(keep, arrived)
    other = move(total, wide, dx=1)
    total, other = yield total, other
    mine = jnp.where(x == 0, jnp.concatenate([total, other]), jnp.concatenate([other, total]))
    mine, theirs = yield mine, move(mine, wide, dc=1)
    return mine, theirs


def totals_body(places, *refs):
    out_ref = refs[-1]
    out_ref[...] = jnp.zeros(out_ref.shape, F32)
    width = out_ref.shape[1]
    for (row, start), ref in zip(places, refs[:-1]):
        for number in range((ref.shape[1] - start) // width):
            at = start + number * width
            value = ref[:, at : at + width].astype(F32)
            if ref.shape[0] > 1:
                value = jnp.sum(value, axis=0, keepdims=True)
            out_ref[row + number : row + number + 1, :] = value


def totals(entries, width):
    arrays = [array for _, array, _ in entries]
    return pl.pallas_call(
        functools.partial(totals_body, [(row, start) for row, _, start in entries]),
        out_shape=jax.ShapeDtypeStruct((24, width), F32),
        in_specs=[vmem()] * len(arrays),
        out_specs=vmem(),
        name="totals",
        cost_estimate=pl.CostEstimate(flops=0, bytes_accessed=24 * width, transcendentals=0),
    )(*arrays)


class Chain:
    def __init__(self, steps):
        self.steps = steps
        self.held = next(steps)
        self.result = None

    def finish(self):
        while self.result is None:
            try:
                self.held = self.steps.send(self.held)
            except StopIteration as stop:
                self.result = stop.value
        return self.result


def frame_steps(part, wide):
    arrived = move(part[1], wide, dy=1)
    kept, arrived = yield part[0], arrived
    line = added(kept, arrived)
    arrived = [move(line[d], wide, dz=d) for d in range(1, NZ)]
    total, arrived = yield line[0], arrived
    total = total.astype(F32)
    for value in arrived:
        total = total + value.astype(F32)
    return total


def back_steps(back, y, wide):
    arrived = move(back[3:].astype(BF16), wide, dy=1)
    arrived, back = yield arrived, back
    arrived = arrived.astype(F32)
    line = [
        back[0] + jnp.where(y == 0, arrived[0], 0.0),
        back[1] + jnp.where(y == 0, arrived[1], arrived[0]),
        back[2] + jnp.where(y == 0, 0.0, arrived[1]),
    ]
    arrived = along_z(line[2].astype(BF16), wide, -1)
    own, step, arrived = yield line[0], line[1], arrived
    arrived = along_z((step + arrived.astype(F32)).astype(BF16), wide, -1)
    own, arrived = yield own, arrived
    return own + arrived.astype(F32)


def small_steps(slab, wide):
    moves = (
        lambda v: [move(v, wide, dc=1)],
        lambda v: [move_mixed(v, wide, 0)],
        lambda v: [move_mixed(v, wide, 1)],
        lambda v: [move(v, wide, dz=d) for d in range(1, NZ)],
    )
    for step in moves:
        slab, arrived = yield slab, step(slab.astype(BF16))
        for value in arrived:
            slab = slab + value.astype(F32)
    return slab


def advance(chains, *values):
    held, values = lax.optimization_barrier(([chain.held for chain in chains], values))
    for chain, kept in zip(chains, held):
        try:
            chain.held = chain.steps.send(kept)
        except StopIteration as stop:
            chain.result = stop.value
    return values[0] if len(values) == 1 else values


def finish_grads(both, shapes, coords):
    c = coords[1]
    mine, theirs = both
    low = jnp.where(c == 0, mine, theirs)
    high = jnp.where(c == 0, theirs, mine)
    shards, cursor = [], 0
    for rows, width in shapes:
        half = width // 2
        blocks = []
        for block in range(rows // 96):
            at = slice(cursor, cursor + half)
            blocks.append(jnp.concatenate([low[:, at], high[:, at]], axis=1))
            cursor += half
        whole = blocks[0] if len(blocks) == 1 else jnp.concatenate(blocks, axis=0)
        shards.append(whole.astype(F32))
    return shards


def per_device(
    tokens,
    frames,
    cotangent,
    item_lengths,
    frame_lengths,
    attn_inputs,
    attn_output,
    cross_queries,
    cross_memory,
    cross_output,
    mlp_inputs,
    mlp_output,
    norm_gains,
    bias_rows,
    mlp_bias,
):
    width = tokens.shape[1]
    tok_rows = tokens.shape[0]
    frame_rows = frames.shape[0]
    hidden_rows = mlp_output.shape[0]
    wide = lax.axis_size("wide")
    me = lax.axis_index("wide").astype(jnp.int32)
    group = lax.axis_index("grp").astype(jnp.int32)
    span = LONGEST // tok_rows
    fast = wide == NZ * NY and span == 4
    x, c, z, y = group // 2, group % 2, me // NY, me % NY
    coords = (x, c, z, y)
    part = width // wide

    self_set = (attn_inputs, attn_output)
    cross_set = (cross_queries, cross_memory, cross_output)
    mlp_set = (mlp_inputs, mlp_output)
    if fast:
        places = jnp.stack(coords).astype(jnp.int32)
        own_self = own_piece(self_set, places)
        self_parts = along_line(own_self, wide)
        line = spread(places, frames, norm_gains, bias_rows, mlp_bias)
        own_cross = own_piece(cross_set, places)
        own_mlp = own_piece(mlp_set, places)
        self_parts, line, own_tokens, own_cross, own_mlp = tied(self_parts, line, tokens, own_cross, own_mlp)
        self_parts = [jnp.stack(self_parts)]
        self_parts += [move(self_parts[0], wide, dy=1), move(self_parts[0], wide, dx=1)]
        lines = [line] + [move(line, wide, dz=-d) for d in range(1, NZ)]
        blocks_mine = [own_tokens, along_z(own_tokens, wide, 1), along_z(own_tokens, wide, 2)]
        payload = collect(places, lines, blocks_mine)
        payload, self_parts, own_cross, own_mlp = tied(payload, self_parts, own_cross, own_mlp)
        got = move(payload, wide, dy=1)
        self_parts.append(move(self_parts[1], wide, dx=1))
        self_theirs = [move(v, wide, dc=1) for v in self_parts[:3]]
        cross_parts = along_line(own_cross, wide)
        cross_parts, self_parts, own_mlp = tied(cross_parts, self_parts, own_mlp)
        cross_parts = [jnp.stack(cross_parts)]
        cross_parts += [move(cross_parts[0], wide, dy=1), move(cross_parts[0], wide, dx=1)]
        self_theirs.append(move(self_parts[3], wide, dc=1))
        mlp_parts = along_line(own_mlp, wide)
        all_frames, normal_window, normed_window, params, self_bias, cross_bias, hidden_bias = prepare(
            lines, blocks_mine, got
        )
        w_in, w_out = assemble(self_set, self_parts + self_theirs, True, places, wide)
        cross_parts, w_in, normed_window = tied(cross_parts, w_in, normed_window)
        cross_parts.append(move(cross_parts[1], wide, dx=1))
        cross_theirs = [move(v, wide, dc=1) for v in cross_parts[:3]]
        gains, biases = params[:3], params[3:13]
        number = jnp.arange(wide, dtype=jnp.int32)
        owner = ((z + number % NZ) % NZ) * NY + (y ^ (number // NZ))
        blocks_at = me - jnp.array([0, 2, 4, 1, 3], jnp.int32)
    else:
        gather = functools.partial(lax.all_gather, axis_name="wide", axis=0, tiled=True)
        window = jnp.concatenate([tokens] + [shifted(tokens, wide, o) for o in range(1, span + 1)])
        blocks_at = me - jnp.arange(span + 1, dtype=jnp.int32)
        all_frames = gather(frames)
        owner = jnp.arange(wide, dtype=jnp.int32)
        small = jnp.concatenate([norm_gains.reshape(-1), bias_rows.reshape(-1), mlp_bias])
        params = gather(small.reshape(1, -1))
        w_in, w_out, w_cross_q, w_memory, w_cross_out = [gather(v) for v in self_set + cross_set]
        w_mlp_in, w_mlp_out = [gather(v) for v in mlp_set]
        gains = params[:, : 3 * part].reshape(wide, 3, part).transpose(1, 0, 2).reshape(3, width).astype(F32)
        biases = params[:, 3 * part : 13 * part].reshape(wide, 10, part).transpose(1, 0, 2)
        biases = biases.reshape(10, width).astype(F32)
        hidden_bias = params[:, 13 * part : 13 * part + hidden_rows].reshape(1, -1).astype(F32)
        zero_row = jnp.zeros((1, width), F32)
        self_bias = jnp.concatenate([zero_row, biases[4:5]], axis=1)
        cross_bias = jnp.concatenate([zero_row, biases[7:8]], axis=1)
        normal_window = norm_parts(window.astype(F32))[0]
        normed_window = (normal_window * gains[:1] + biases[:1]).astype(BF16)
    frame_pos = (owner[:, None] * frame_rows + jnp.arange(frame_rows, dtype=jnp.int32)).reshape(1, -1)
    key_pos = (blocks_at[:, None] * tok_rows + jnp.arange(tok_rows, dtype=jnp.int32)).reshape(1, -1)

    def gain(row):
        return gains[row : row + 1]

    def bias(row):
        return biases[row : row + 1]

    info = me.reshape(1)

    def swapped(parts):
        theirs = move(jnp.concatenate(parts), wide, dc=1)
        found, cursor = [], 0
        for value in parts:
            found.append(theirs[cursor : cursor + value.shape[0]])
            cursor += value.shape[0]
        return found

    def halves(values):
        half = values[0].shape[1] // 2
        mine = [lax.dynamic_slice_in_dim(v, c * half, half, 1) for v in values]
        theirs = swapped([lax.dynamic_slice_in_dim(v, (1 - c) * half, half, 1) for v in values])
        return [jnp.concatenate(pair) for pair in zip(mine, theirs)]

    def doubled(values):
        return [jnp.concatenate(pair) for pair in zip(values, swapped(values))]

    def weight(left, right):
        grad = dot_tn(left, right).astype(BF16)
        return grad.reshape(wide, -1, 96, grad.shape[1])

    def blocks(*grads):
        return [grad[:, i] for grad in grads for i in range(grad.shape[1])]

    inputs = tokens.astype(F32)
    normed_one = normed_window[:tok_rows]
    query = (dot(normed_one, w_in[:, :width]) + bias(3)).astype(BF16)
    self_kv = (dot(normed_window, w_in[:, width:]) + self_bias).astype(BF16)
    tables = (info, item_lengths, frame_lengths)
    if fast:
        cross_parts, mlp_parts, self_kv = tied(cross_parts, mlp_parts, self_kv)
        cross_theirs.append(move(cross_parts[3], wide, dc=1))
        mlp_parts = [jnp.stack(mlp_parts)]
        mlp_parts += [move_mixed(mlp_parts[0], wide, 0), move_mixed(mlp_parts[0], wide, 1)]
        w_cross_q, w_memory, w_cross_out = assemble(cross_set, cross_parts + cross_theirs, True, places, wide)
    attended = attention_forward("self", *tables, key_pos, query, self_kv)
    after_one = inputs + dot(attended, w_out) + bias(5)
    normed_two = norm_apply(after_one, gain(1), bias(1)).astype(BF16)
    cross_q = (dot(normed_two, w_cross_q) + bias(6)).astype(BF16)
    memory = (dot(all_frames, w_memory) + cross_bias).astype(BF16)
    if fast:
        mlp_parts, memory = tied(mlp_parts, memory)
        mlp_parts.append(move_mixed(mlp_parts[1], wide, 1))
        mlp_theirs = [move(v, wide, dc=1) for v in mlp_parts[:3]]
    cross_att = attention_forward("cross", *tables, frame_pos, cross_q, memory)
    if fast:
        mlp_theirs.append(move(mlp_parts[3], wide, dc=1))
        w_mlp_in, w_mlp_out = assemble(mlp_set, mlp_parts + mlp_theirs, False, places, wide)
    after_two = after_one + dot(cross_att, w_cross_out) + bias(8)
    normed_three = norm_apply(after_two, gain(2), bias(2)).astype(BF16)
    pre_act = dot(normed_three, w_mlp_in) + hidden_bias
    exact_gelu = functools.partial(jax.nn.gelu, approximate=False)
    hidden = exact_gelu(pre_act).astype(BF16)

    grad_out = cotangent.astype(F32)
    grad_hidden = dot_nt(cotangent, w_mlp_out)
    grad_pre = jax.vjp(exact_gelu, pre_act)[1](grad_hidden)[0].astype(BF16)
    if fast:
        window_two, frames_two, attended_two, two_two, cross_att_two, three_two = doubled(
            [normed_window, all_frames, attended, normed_two, cross_att, normed_three]
        )
        rows_two = normed_window.shape[0]
        one_two = jnp.concatenate([window_two[:tok_rows], window_two[rows_two : rows_two + tok_rows]])
        (hidden_two,) = doubled([hidden])
        (out_half,) = halves([cotangent])
        chain_out = Chain(scatter_steps(blocks(weight(hidden_two, out_half)), coords, wide))
        grad_pre = advance([chain_out], grad_pre)
        (pre_half,) = halves([grad_pre])
        chain_in = Chain(scatter_steps(blocks(weight(three_two, pre_half)), coords, wide))
        grad_pre = advance([chain_in], grad_pre)
    grad_three, gain_three, shift_three = norm_back(after_two, gain(2), dot_nt(grad_pre, w_mlp_in))
    grad_after_two = grad_out + grad_three
    grad_cross_branch = grad_after_two.astype(BF16)
    grad_cross_att = dot_nt(grad_cross_branch, w_cross_out).astype(BF16)
    grad_cross_q, grad_memory = attention_backward(
        "cross", *tables, frame_pos, cross_q, memory, grad_cross_att
    )
    if fast:
        grad_cross_q, grad_memory = advance([chain_out], grad_cross_q, grad_memory)
    grad_two, gain_two, shift_two = norm_back(after_one, gain(1), dot_nt(grad_cross_q, w_cross_q))
    grad_after_one = grad_after_two + grad_two
    grad_self_branch = grad_after_one.astype(BF16)
    if fast:
        grad_self_branch = advance([chain_in], grad_self_branch)
    grad_attended = dot_nt(grad_self_branch, w_out).astype(BF16)

    frame_part = dot_nt(grad_memory, w_memory)
    if fast:
        branch_half, cross_half, keys_half, values_half, self_half = halves(
            [grad_cross_branch, grad_cross_q, grad_memory[:, :width], grad_memory[:, width:], grad_self_branch]
        )
        pieces = blocks(
            weight(frames_two, keys_half),
            weight(frames_two, values_half),
            weight(cross_att_two, branch_half),
            weight(two_two, cross_half),
            weight(attended_two, self_half),
        )
        chain_cross = Chain(scatter_steps(pieces, coords, wide))
        frame_part = frame_part.astype(BF16).reshape(NY, NZ, frame_rows, width)
        chain_frames = Chain(frame_steps(frame_part, wide))
        grad_attended = advance([chain_out, chain_cross], grad_attended)
    else:
        grad_frames = lax.psum_scatter(frame_part, "wide", scatter_dimension=0, tiled=True)
    grad_query, grad_kv = attention_backward("self", *tables, key_pos, query, self_kv, grad_attended)
    if fast:
        grad_query, grad_kv = advance([chain_cross, chain_out], grad_query, grad_kv)
        query_half, keys_half, values_half = halves([grad_query, grad_kv[:, :width], grad_kv[:, width:]])
        grad_in = [weight(one_two, query_half), weight(window_two, keys_half), weight(window_two, values_half)]
        chain_self = Chain(scatter_steps(blocks(*grad_in), coords, wide))
        grad_kv, grad_pre, hidden = advance(
            [chain_self, chain_in, chain_out, chain_frames], grad_kv, grad_pre, hidden
        )

    window_part = dot_nt(grad_kv, w_in[:, width:])
    own_part = window_part[:tok_rows] + dot_nt(grad_query, w_in[:, :width])
    window_part = jnp.concatenate([own_part, window_part[tok_rows:]])
    gain_one = jnp.sum(window_part * normal_window, axis=0, keepdims=True)
    shift_one = jnp.sum(window_part, axis=0, keepdims=True)
    last_gain = gain(0)
    if fast:
        back = window_part.reshape(5, tok_rows, width)
        chain_back = Chain(back_steps(back, y, wide))
        rows = [
            (0, gain_one, 0),
            (1, gain_two, 0),
            (2, gain_three, 0),
            (3, shift_one, 0),
            (4, shift_two, 0),
            (5, shift_three, 0),
            (6, grad_query, 0),
            (7, grad_kv, width),
            (8, grad_self_branch, 0),
            (9, grad_cross_q, 0),
            (10, grad_memory, width),
            (11, grad_cross_branch, 0),
            (12, cotangent, 0),
            (13, grad_pre, 0),
        ]
        chain_small = Chain(small_steps(totals(rows, width), wide))
        last_gain, hidden = advance([chain_self, chain_cross, chain_in, chain_small], last_gain, hidden)
        last_gain = advance([chain_self, chain_cross, chain_in, chain_back, chain_small, chain_out], last_gain)
        last_gain = advance([chain_self, chain_cross, chain_back, chain_small, chain_in, chain_frames], last_gain)
        last_gain = advance([chain_self, chain_cross, chain_small], last_gain)
        last_gain = advance([chain_self, chain_back], last_gain)
        grad_one = chain_back.finish()
        grad_frames = chain_frames.finish()
        small = chain_small.finish()
    else:
        grad_one = own_part
        for o in range(1, span + 1):
            block = window_part[o * tok_rows : (o + 1) * tok_rows]
            grad_one = grad_one + shifted(block.astype(BF16), wide, -o).astype(F32)
    block_output = (after_two + dot(hidden, w_mlp_out) + bias(9)).astype(BF16)
    grad_tokens = grad_after_one + norm_back(inputs, last_gain, grad_one)[0]

    if fast:
        small_hidden = pick(small[13:17], me // NY, 0)
        small_hidden = lax.dynamic_slice_in_dim(small_hidden, (me % NY) * hidden_rows, hidden_rows, 0)
        small = lax.dynamic_slice_in_dim(small, me * part, part, 1)
        square = (part, width)
        (g_mlp_in,) = finish_grads(chain_in.finish(), [mlp_inputs.shape], coords)
        (g_mlp_out,) = finish_grads(chain_out.finish(), [mlp_output.shape], coords)
        g_memory_k, g_memory_v, g_cross_out, g_cross_q, g_out = finish_grads(
            chain_cross.finish(), [square] * 5, coords
        )
        g_in_q, g_in_k, g_in_v = finish_grads(chain_self.finish(), [square] * 3, coords)
        g_memory = jnp.concatenate([g_memory_k, g_memory_v], axis=1)
        g_in = jnp.concatenate([g_in_q, g_in_k, g_in_v], axis=1)
        rows_all, g_bias = small[:13], small_hidden
    else:

        def weight_sum(left, right):
            grad = lax.psum_scatter(dot_tn(left, right), "wide", scatter_dimension=0, tiled=True)
            return lax.psum(grad.astype(BF16), "grp").astype(F32)

        def total(value):
            return jnp.sum(value.astype(F32), axis=0, keepdims=True)

        rows = [
            gain_one,
            gain_two,
            gain_three,
            shift_one,
            shift_two,
            shift_three,
            total(grad_query),
            total(grad_kv[:, width:]),
            total(grad_self_branch),
            total(grad_cross_q),
            total(grad_memory[:, width:]),
            total(grad_cross_branch),
            total(grad_out),
        ]
        g_in = jnp.concatenate(
            [weight_sum(normed_one, grad_query), weight_sum(normed_window, grad_kv)], axis=1
        )
        g_out = weight_sum(attended, grad_self_branch)
        g_cross_q = weight_sum(normed_two, grad_cross_q)
        g_memory = weight_sum(all_frames, grad_memory)
        g_cross_out = weight_sum(cross_att, grad_cross_branch)
        g_mlp_in = weight_sum(normed_three, grad_pre)
        g_mlp_out = weight_sum(hidden, cotangent)
        small = lax.psum(jnp.concatenate(rows), BOTH)
        rows_all = lax.dynamic_slice_in_dim(small, me * part, part, 1)
        g_bias = lax.psum(total(grad_pre).reshape(-1), BOTH)
        g_bias = lax.dynamic_slice_in_dim(g_bias, me * hidden_rows, hidden_rows, 0)
    return (
        block_output,
        grad_tokens,
        grad_frames,
        g_in,
        g_out,
        g_cross_q,
        g_memory,
        g_cross_out,
        g_mlp_in,
        g_mlp_out,
        rows_all[:3],
        rows_all[3:],
        g_bias,
    )


def solution(mesh):
    rows = P(BOTH, None)
    weight = P("wide", None)
    columns = P(None, "wide")
    return jax.shard_map(
        per_device,
        mesh=mesh,
        in_specs=(rows,) * 3 + (P("grp", None),) * 2 + (weight,) * 7 + (columns, columns, P("wide")),
        out_specs=(rows,) * 3 + (weight,) * 7 + (columns, columns, P("wide")),
        check_vma=False,
    )
```
